256 devices in a mesh: gx: 16 (over z_hi, y), gz: 16 (over z_lo, x, core).
Axes of the slice: x: 4, y: 4, z: 8 (z_hi: 4, z_lo: 2; z = z_hi * 2 + z_lo), core: 2. Of those that a mesh axis runs over, the one named last changes fastest.
Arguments:
- rho_prev: float32 [128, 512, 512], P('gz', 'gx'), may hold values from 0.3 to 8.2, as said below
- potential: float32 [128, 512, 512], P('gz', 'gx'), may hold values from 0 to 1.5
Outputs:
- rho_next: float32 [128, 512, 512], P('gz', 'gx')
- mass_ratio: float32 [1], replicated
The draws below stay inside these ranges and needn't reach their ends.
Inputs may be any that keep to these rules, and one draw needn't show every extreme that they name: `rho_prev`: strictly positive in every cell.
All inputs are finite; a program needn't handle non-finite values.
Results may differ from the reference program's by a relative error of at most 0.0001.
Values sent between devices are 32-bit elements; how exact they have to be, the bound alone decides.
No kernel may reach another device: no remote copies, remote signals or barrier semaphores. Data moves between devices by JAX's collectives and lax.ppermute only.
A program may use at most 64 MiB of HBM per device.

```python
import jax
import jax.numpy as jnp
from jax import lax

NY = 512
HALF = 8
ITERS = 3
NEWTON = 6
NX = 512
NZ = 128


def draw_rho_prev(key, part):
    rough = jax.random.uniform(key, (NZ, NX, NY), jnp.float32, -1.0, 1.0)
    along_x = jnp.arange(NX).astype(jnp.float32) / (NX - 1)
    along_z = jnp.arange(NZ).astype(jnp.float32) / (NZ - 1)
    envelope = 1.0 + along_x[None, :, None] + along_z[:, None, None]
    return jnp.exp(rough) * envelope


def block_scale(key, dims, cuts, low, largest):
    level, own = 1.0, jax.random.fold_in(key, 6)
    for axis_at, blocks in cuts:
        heights = jnp.exp(jax.random.uniform(jax.random.fold_in(own, axis_at), (blocks,), jnp.float32, low / len(cuts), largest / len(cuts)))
        level = level * jnp.repeat(heights, dims[axis_at] // blocks).reshape([-1 if axis == axis_at else 1 for axis in range(len(dims))])
    return level


def setup_inputs(seed: int = 0) -> dict:
    key_of = jax.random.split(jax.random.key(seed), 3)
    return {
        "rho_prev": draw_rho_prev(jax.random.fold_in(key_of[2], 71), 0),
        "potential": jnp.clip(1.5 * jax.random.uniform(key_of[1], (NZ, NX, NY), jnp.float32) ** block_scale(key_of[1], (NZ, NX, NY), ((0, 16), (1, 16)), -0.2, 0.2), 0.0, 1.5),
    }


def weight_table():
    offsets = jnp.arange(-HALF, HALF + 1).astype(jnp.float32)
    raw = jnp.exp(-2.0 * offsets * offsets / (HALF * HALF))
    return raw / jnp.sum(raw)


def convolve_axis(field, axis):
    weights = weight_table()
    length = field.shape[axis]
    widths = [(0, 0)] * field.ndim
    widths[axis] = (HALF, HALF)
    padded = jnp.pad(field, widths)
    total = jnp.zeros_like(field)
    for shift in range(2 * HALF + 1):
        piece = lax.slice_in_dim(padded, shift, shift + length, axis=axis)
        total = total + weights[shift] * piece
    return total


def heat(field):
    return convolve_axis(convolve_axis(convolve_axis(field, 0), 1), 2)


def prox(target):
    current = target
    for turn in range(NEWTON):
        grown = 0.5 * jnp.exp(current)
        current = current - (current + grown - target) / (1.0 + grown)
    return jnp.exp(current)


def reference(rho_prev, potential):
    scaling = jnp.ones_like(rho_prev)
    rho = scaling
    for sweep in range(ITERS):
        dual = rho_prev / heat(scaling)
        spread = heat(dual)
        target = jnp.log(scaling * spread) - potential
        rho = prox(target)
        scaling = rho / spread
    mass_prev = jnp.sum(rho_prev)
    mass_new = jnp.sum(rho)
    mass_ratio = jnp.reshape(mass_new / mass_prev, (1,))
    return rho * (mass_prev / mass_new), mass_ratio
```

```python
import functools

import jax
import jax.numpy as jnp
import numpy as np
from jax import lax
from jax.experimental import pallas as pl
from jax.experimental.pallas import tpu as pltpu
from jax.sharding import PartitionSpec as P

HALF = 8
ITERS = 3
NEWTON = 6
LANES = 128


def weight(gap):
    offsets = np.arange(-HALF, HALF + 1)
    total = float(np.sum(np.exp(-2.0 * offsets * offsets / (HALF * HALF))))
    gap = gap.astype(jnp.float32)
    raw = jnp.exp(-2.0 * gap * gap / (HALF * HALF)) / total
    return jnp.where(jnp.abs(gap) <= HALF, raw, 0.0)


def split(value):
    high = value.astype(jnp.bfloat16)
    return high, (value - high.astype(jnp.float32)).astype(jnp.bfloat16)


def dot3(left, right):
    dot = functools.partial(jnp.dot, preferred_element_type=jnp.float32)
    return dot(left[0], right[0]) + (dot(left[0], right[1]) + dot(left[1], right[0]))


def iota(shape, dim):
    return lax.broadcasted_iota(jnp.int32, shape, dim)


def swap(value, axis, first):
    size = lax.axis_size(axis)
    pairs = [(i, i + 1) for i in range(first, size - 1, 2)]
    return lax.ppermute(value, axis, pairs + [(j, i) for i, j in pairs])


def x_matrix(depth, width, even):
    rows = depth * width
    shape = (rows, rows + 2 * depth * HALF)
    row, col = iota(shape, 0), iota(shape, 1)
    halo = col - rows
    side = halo // (depth * HALF)
    halo = halo % (depth * HALF)
    own = col < rows
    after = jnp.where(side == 0, even, 1 - even) == 1
    col_z = jnp.where(own, col // width, halo // HALF)
    col_x = jnp.where(own, col % width, halo % HALF + jnp.where(after, width, -HALF))
    return split(jnp.where(row // width == col_z, weight(row % width - col_x), 0.0))


def z_matrix(depth, width, even):
    rows = depth * width
    shape = (rows, 3 * rows)
    row, col = iota(shape, 0), iota(shape, 1)
    block, cell = col // rows, col % rows
    after = jnp.where(block == 1, 1 - even, even) == 1
    shift = jnp.where(block == 0, 0, jnp.where(after, depth, -depth))
    gap = row // width - cell // width - shift
    return split(jnp.where(row % width == cell % width, weight(gap), 0.0))


def y_matrix(length):
    shape = (length, length)
    return split(weight(iota(shape, 0) - iota(shape, 1)))


def edges(even, value, first_ref, second_ref, depth, width):
    shaped = value.reshape(depth, width, -1)
    low, high = shaped[:, :HALF], shaped[:, width - HALF :]
    first_ref[...] = jnp.where(even == 1, high, low).reshape(first_ref.shape)
    second_ref[...] = jnp.where(even == 1, low, high).reshape(second_ref.shape)


def lane_sums(value):
    rows = jnp.sum(value, axis=0, keepdims=True)
    return sum(rows[:, i : i + LANES] for i in range(0, rows.shape[1], LANES))


def xy_kernel(own, first, second, x_high, x_low, y_high, y_low, out, high, low):
    at = 0
    for part in (own, first, second):
        span = pl.ds(at, part.shape[0])
        high[span], low[span] = split(part[...])
        at += part.shape[0]
    along_x = dot3((x_high[...], x_low[...]), (high[...], low[...]))
    out[...] = dot3(split(along_x), (y_high[...], y_low[...]))


def along_z(own, first, second, z_high, z_low, high, low):
    at = 0
    for part in (own, first, second):
        span = pl.ds(at, part.shape[0])
        high[span], low[span] = split(part[...])
        at += part.shape[0]
    return dot3((z_high[...], z_low[...]), (high[...], low[...]))


def dual_kernel(depth, width, even, own, first, second, z_high, z_low, rho_prev, out, edge0, edge1, high, low):
    dual = rho_prev[...] / along_z(own, first, second, z_high, z_low, high, low)
    out[...] = dual
    edges(even[0], dual, edge0, edge1, depth, width)


def prox(target):
    current = target
    for _ in range(NEWTON):
        grown = 0.5 * jnp.exp(current)
        current = (grown * (current - 1.0) + target) / (1.0 + grown)
    return jnp.exp(current)


def scaling_kernel(depth, width, started, even, own, first, second, z_high, z_low, potential, *rest):
    if started:
        scaling_ref, *rest = rest
    out, edge0, edge1, high, low = rest
    spread = along_z(own, first, second, z_high, z_low, high, low)
    inner = scaling_ref[...] * spread if started else spread
    scaling = prox(jnp.log(inner) - potential[...]) / spread
    out[...] = scaling
    edges(even[0], scaling, edge0, edge1, depth, width)


def last_kernel(own, first, second, z_high, z_low, potential, scaling, rho_prev, out, sums, high, low):
    spread = along_z(own, first, second, z_high, z_low, high, low)
    rho = prox(jnp.log(scaling[...] * spread) - potential[...])
    out[...] = rho
    sums[:, :LANES] = lane_sums(rho_prev[...])
    sums[:, LANES:] = lane_sums(rho)


def first_kernel(depth, width, even, rho_prev, row_mass, col_mass, out, edge0, edge1):
    dual = rho_prev[...] / (row_mass[...] * col_mass[...])
    out[...] = dual
    edges(even[0], dual, edge0, edge1, depth, width)


def scale_kernel(rho, sums, out, ratio):
    totals = jnp.sum(sums[...], axis=0, keepdims=True)
    mass_prev, mass_new = jnp.sum(totals[:, :LANES]), jnp.sum(totals[:, LANES:])
    ones = jnp.ones((1, LANES), jnp.float32)
    prev, new = mass_prev * ones, mass_new * ones
    ratio[...] = new / prev
    out[...] = rho[...] * (prev / new)[:, :1]


def call(kernel, inputs, shapes, scratch=(), scalars=0):
    specs = [pl.BlockSpec(memory_space=pltpu.SMEM)] * scalars
    specs += [pl.BlockSpec(memory_space=pltpu.VMEM)] * (len(inputs) - scalars)
    return pl.pallas_call(
        kernel,
        out_shape=[jax.ShapeDtypeStruct(shape, jnp.float32) for shape in shapes],
        in_specs=specs,
        out_specs=[pl.BlockSpec(memory_space=pltpu.VMEM)] * len(shapes),
        scratch_shapes=scratch,
        compiler_params=pltpu.CompilerParams(vmem_limit_bytes=24 << 20),
    )(*inputs)


def edge_mass(first, count, whole):
    cell = first + iota((count, 2 * HALF + 1), 0)
    gap = iota((count, 2 * HALF + 1), 1) - HALF
    inside = (cell + gap >= 0) & (cell + gap < whole)
    return jnp.sum(jnp.where(inside, weight(gap), 0.0), axis=1)


def body(rho_prev, potential):
    depth, width, length = rho_prev.shape
    rows = depth * width
    at_x, at_z = lax.axis_index("gx"), lax.axis_index("gz")
    whole_x, whole_z = width * lax.axis_size("gx"), depth * lax.axis_size("gz")
    even_x, even_z = 1 - at_x % 2, 1 - at_z % 2
    even = jnp.reshape(even_x, (1,)).astype(jnp.int32)
    rho_prev, potential = rho_prev.reshape(rows, length), potential.reshape(rows, length)
    x_table = x_matrix(depth, width, even_x)
    z_table = z_matrix(depth, width, even_z)
    y_table = y_matrix(length)
    full, edge = (rows, length), (depth * HALF, length)

    def convolved(field, edge0, edge1):
        second = swap(edge1, "gx", 1)
        first = swap(edge0, "gx", 0)
        scratch = [pltpu.VMEM((rows + 2 * depth * HALF, length), jnp.bfloat16)] * 2
        (own,) = call(xy_kernel, (field, first, second, *x_table, *y_table), [full], scratch)
        far = swap(own, "gz", 1)
        near = swap(own, "gz", 0)
        return own, far, near, *z_table

    row_mass = edge_mass(at_z * depth, depth, whole_z)[:, None] * edge_mass(at_x * width, width, whole_x)[None, :]
    col_mass = edge_mass(0, length, length)[None, :]
    scratch = [pltpu.VMEM((3 * rows, length), jnp.bfloat16)] * 2

    def with_sizes(kernel, *more):
        return functools.partial(kernel, depth, width, *more)

    field = call(with_sizes(first_kernel), (even, rho_prev, row_mass.reshape(rows, 1), col_mass), [full, edge, edge], scalars=1)
    scaling = None
    for sweep in range(ITERS):
        if sweep:
            field = call(with_sizes(dual_kernel), (even, *convolved(*field), rho_prev), [full, edge, edge], scratch, 1)
        spread = convolved(*field)
        if sweep == ITERS - 1:
            rho, sums = call(last_kernel, (*spread, potential, scaling, rho_prev), [full, (1, 2 * LANES)], scratch)
        else:
            more = () if scaling is None else (scaling,)
            field = call(with_sizes(scaling_kernel, bool(more)), (even, *spread, potential, *more), [full, edge, edge], scratch, 1)
            scaling = field[0]
    everyone = lax.axis_size("gx") * lax.axis_size("gz")
    sums = jnp.broadcast_to(sums[None], (everyone, 1, 2 * LANES))
    sums = lax.all_to_all(sums, ("gx", "gz"), 0, 0, tiled=True).reshape(everyone, 2 * LANES)
    rho_next, ratio = call(scale_kernel, (rho, sums), [full, (1, LANES)])
    return rho_next.reshape(depth, width, length), ratio[0, :1]


def solution(mesh):
    return jax.shard_map(
        body,
        mesh=mesh,
        in_specs=(P("gz", "gx", None), P("gz", "gx", None)),
        out_specs=(P("gz", "gx", None), P()),
        check_vma=False,
    )
```

```python
import functools

import jax
import jax.numpy as jnp
import numpy as np
from jax import lax
from jax.experimental import pallas as pl
from jax.experimental.pallas import tpu as pltpu
from jax.sharding import PartitionSpec as P

HALF = 8
ITERS = 3
NEWTON = 6
LANES = 128


EDGE, INNER = (0, 3), (1, 2)


def scale():
    offsets = np.arange(-HALF, HALF + 1)
    return float(np.sum(np.exp(-2.0 * offsets * offsets / (HALF * HALF))))


def weight(gap):
    gap = gap.astype(jnp.float32)
    raw = jnp.exp(-2.0 * gap * gap / (HALF * HALF)) / scale()
    return jnp.where(jnp.abs(gap) <= HALF, raw, 0.0)


def inside_mass(cell, whole):
    total = jnp.zeros(cell.shape, jnp.float32)
    for gap in range(-HALF, HALF + 1):
        share = float(np.exp(-2.0 * gap * gap / (HALF * HALF)) / scale())
        total += jnp.where((cell + gap >= 0) & (cell + gap < whole), share, 0.0)
    return total


def split(value):
    high = value.astype(jnp.bfloat16)
    return high, (value - high.astype(jnp.float32)).astype(jnp.bfloat16)


def dot3(left, right):
    dot = functools.partial(jnp.dot, preferred_element_type=jnp.float32)
    return dot(left[0], right[0]) + (dot(left[0], right[1]) + dot(left[1], right[0]))


def iota(shape, dim):
    return lax.broadcasted_iota(jnp.int32, shape, dim)


def swap(value, axis, first):
    size = lax.axis_size(axis)
    pairs = [(i, i + 1) for i in range(first, size - 1, 2)]
    return lax.ppermute(value, axis, pairs + [(j, i) for i, j in pairs])


def group(ref, at):
    return ref[:, at * HALF : (at + 1) * HALF, :]


def groups(ref, which):
    return jnp.concatenate([group(ref, at).reshape(-1, ref.shape[2]) for at in which], axis=0)


def tables_kernel(depth, where, z_high, z_low, x_high, x_low, side_high, side_low, y_high, y_low):
    even = where[1]
    shape = z_high.shape
    rows = shape[0]
    row, col = iota(shape, 0), iota(shape, 1)
    block, cell = col // rows, col % rows
    far = jnp.where(even == 1, -depth, depth)
    gap = row // HALF - cell // HALF - jnp.where(block == 0, 0, jnp.where(block == 1, far, -far))
    z_high[...], z_low[...] = split(jnp.where(row % HALF == cell % HALF, weight(gap), 0.0))
    shape = x_high.shape
    row, col = iota(shape, 0), iota(shape, 1)
    gap = row % HALF - col % HALF + HALF * (row // rows - col // rows)
    same = row % rows // HALF == col % rows // HALF
    x_high[...], x_low[...] = split(jnp.where(same, weight(gap), 0.0))
    shape = side_high.shape
    row, col = iota(shape, 0), iota(shape, 1)
    gap = row % HALF - col % HALF + jnp.where(row < rows, HALF, -HALF)
    side_high[...], side_low[...] = split(jnp.where(row % rows // HALF == col // HALF, weight(gap), 0.0))
    shape = y_high.shape
    y_high[...], y_low[...] = split(weight(iota(shape, 0) - iota(shape, 1)))


def first_kernel(sizes, where, rho_prev, edge, inner):
    depth, width, length = rho_prev.shape
    whole_x, whole_z = sizes
    mass_z = inside_mass(where[3] + iota((depth, LANES), 0), whole_z)
    mass_y = inside_mass(iota((1, length), 1), length)
    rows = depth * HALF
    for ref, which in ((edge, EDGE), (inner, INNER)):
        for place, at in enumerate(which):
            mass_x = inside_mass(where[2] + at * HALF + iota((HALF, LANES), 0), whole_x)
            for z in range(depth):
                mass = (mass_x[:, :1] * mass_z[z : z + 1, :1]) * mass_y
                start = place * rows + z * HALF
                ref[start : start + HALF] = rho_prev[z, at * HALF : (at + 1) * HALF, :] / mass


def zy(own, far, near, z_high, z_low, y_high, y_low, high, low):
    rows = z_high.shape[0]
    results = []
    for place in range(2):
        span = slice(place * rows, (place + 1) * rows)
        for block, ref in enumerate((own, far, near)):
            to = slice((3 * place + block) * rows, (3 * place + block + 1) * rows)
            high[to], low[to] = split(ref[span])
        at = slice(3 * place * rows, 3 * (place + 1) * rows)
        results.append(dot3((z_high[...], z_low[...]), (high[at], low[at])))
    return dot3(split(jnp.concatenate(results, axis=0)), (y_high[...], y_low[...]))


def edge_kernel(where, own, far, near, z_high, z_low, y_high, y_low, send1, send0, high, low):
    value = zy(own, far, near, z_high, z_low, y_high, y_low, high, low)
    rows = value.shape[0] // 2
    before, after = value[:rows], value[rows:]
    send0[...] = jnp.where(where[0] == 1, after, before)
    send1[...] = jnp.where(where[0] == 1, before, after)


def prox(target):
    current = target
    for _ in range(NEWTON):
        grown = 0.5 * jnp.exp(current)
        current = (grown * (current - 1.0) + target) / (1.0 + grown)
    return jnp.exp(current)


def finish(kind, value, which, whole, scaling):
    if kind == "dual":
        return groups(whole, which) / value
    inner = value if scaling is None else scaling[...] * value
    rho = prox(jnp.log(inner) - groups(whole, which))
    return rho if kind == "last" else rho / value


def lane_sums(value):
    rows = jnp.sum(value, axis=0, keepdims=True)
    return sum(rows[:, i : i + LANES] for i in range(0, rows.shape[1], LANES))


def inner_kernel(kind, started, where, send1, send0, own, far, near, z_high, z_low, y_high, y_low, x_high, x_low, whole, *rest):
    scaling = None
    if started:
        scaling, *rest = rest
    if kind == "last":
        rho_prev, out, part, sums, high, low, zy_high, zy_low = rest
    else:
        out, part, high, low, zy_high, zy_low = rest
    rows = z_high.shape[0]
    value = zy(own, far, near, z_high, z_low, y_high, y_low, high, low)
    before = jnp.where(where[0] == 1, send1[...], send0[...])
    after = jnp.where(where[0] == 1, send0[...], send1[...])
    zy_high[:rows], zy_low[:rows] = split(before)
    zy_high[rows : 3 * rows], zy_low[rows : 3 * rows] = split(value)
    zy_high[3 * rows :], zy_low[3 * rows :] = split(after)
    along_x = dot3((x_high[...], x_low[...]), (zy_high[...], zy_low[...]))
    part[:rows], part[rows:] = along_x[:rows], along_x[3 * rows :]
    result = finish(kind, along_x[rows : 3 * rows], INNER, whole, scaling)
    out[...] = result
    if kind == "last":
        depth, width, length = rho_prev.shape
        sums[:, :LANES] = lane_sums(rho_prev[...].reshape(depth * width, length))
        sums[:, LANES:] = lane_sums(result)


def outer_kernel(kind, started, where, part, recv1, recv0, side_high, side_low, whole, *rest):
    scaling = None
    if started:
        scaling, *rest = rest
    if kind == "last":
        sums_inner, out, sums = rest
    else:
        (out,) = rest
    rows = recv0.shape[0]
    before = split(jnp.where(where[0] == 1, recv1[...], recv0[...]))
    after = split(jnp.where(where[0] == 1, recv0[...], recv1[...]))
    first = part[:rows] + dot3((side_high[:rows], side_low[:rows]), before)
    second = part[rows:] + dot3((side_high[rows:], side_low[rows:]), after)
    result = finish(kind, jnp.concatenate([first, second], axis=0), EDGE, whole, scaling)
    out[...] = result
    if kind == "last":
        sums[...] = sums_inner[...]
        sums[:, LANES:] += lane_sums(result)


def scale_kernel(edge, inner, sums, out, ratio):
    totals = jnp.sum(sums[...], axis=0, keepdims=True)
    mass_prev, mass_new = jnp.sum(totals[:, :LANES]), jnp.sum(totals[:, LANES:])
    ones = jnp.ones((1, LANES), jnp.float32)
    prev, new = mass_prev * ones, mass_new * ones
    ratio[...] = new / prev
    factor = (prev / new)[:, :1]
    depth, width, length = out.shape
    rows = depth * HALF
    for ref, which in ((edge, EDGE), (inner, INNER)):
        for place, at in enumerate(which):
            value = ref[place * rows : (place + 1) * rows] * factor
            out[:, at * HALF : (at + 1) * HALF, :] = value.reshape(depth, HALF, length)


def call(kernel, inputs, shapes, scratch=(), scalars=1, dtype=jnp.float32):
    specs = [pl.BlockSpec(memory_space=pltpu.SMEM)] * scalars
    specs += [pl.BlockSpec(memory_space=pltpu.VMEM)] * (len(inputs) - scalars)
    return pl.pallas_call(
        kernel,
        out_shape=[jax.ShapeDtypeStruct(shape, dtype) for shape in shapes],
        in_specs=specs,
        out_specs=[pl.BlockSpec(memory_space=pltpu.VMEM)] * len(shapes),
        scratch_shapes=scratch,
        compiler_params=pltpu.CompilerParams(vmem_limit_bytes=20 << 20),
    )(*inputs)


def body(rho_prev, potential):
    depth, width, length = rho_prev.shape
    at_x, at_z = lax.axis_index("gx"), lax.axis_index("gz")
    size_x, size_z = lax.axis_size("gx"), lax.axis_size("gz")
    where = jnp.stack([1 - at_x % 2, 1 - at_z % 2, at_x * width, at_z * depth]).astype(jnp.int32)
    rows = depth * HALF
    one, two = (rows, length), (2 * rows, length)
    zy_scratch = [pltpu.VMEM((6 * rows, length), jnp.bfloat16)] * 2
    x_scratch = [pltpu.VMEM((4 * rows, length), jnp.bfloat16)] * 2

    first = functools.partial(first_kernel, (width * size_x, depth * size_z))
    edge, inner = call(first, (where, rho_prev), [two, two])
    table_shapes = [(rows, 3 * rows), (4 * rows, 4 * rows), (2 * rows, rows), (length, length)]
    doubled = [shape for shape in table_shapes for _ in range(2)]
    tables = call(functools.partial(tables_kernel, depth), (where,), doubled, dtype=jnp.bfloat16)
    z_table, x_table, side_table, y_table = (tuple(tables[i : i + 2]) for i in range(0, 8, 2))

    def heat_step(kind, edge, inner, whole, scaling):
        far_edge, near_edge = swap(edge, "gz", 1), swap(edge, "gz", 0)
        far_inner, near_inner = swap(inner, "gz", 1), swap(inner, "gz", 0)
        sends = call(edge_kernel, (where, edge, far_edge, near_edge, *z_table, *y_table), [one, one], zy_scratch)
        recv1, recv0 = swap(sends[0], "gx", 1), swap(sends[1], "gx", 0)
        started, last = scaling is not None, kind == "last"
        inputs = (where, *sends, inner, far_inner, near_inner, *z_table, *y_table, *x_table, whole)
        more = ((scaling[1],) if started else ()) + ((rho_prev,) if last else ())
        shapes = [two, two] + ([(1, 2 * LANES)] if last else [])
        new_inner, part, *sums = call(
            functools.partial(inner_kernel, kind, started), inputs + more, shapes, zy_scratch + x_scratch
        )
        more = ((scaling[0],) if started else ()) + tuple(sums)
        shapes = [two] + ([(1, 2 * LANES)] if last else [])
        new_edge, *sums = call(
            functools.partial(outer_kernel, kind, started),
            (where, part, recv1, recv0, *side_table, whole, *more),
            shapes,
        )
        return new_edge, new_inner, *sums

    scaling = None
    for sweep in range(ITERS):
        if sweep:
            edge, inner = heat_step("dual", edge, inner, rho_prev, None)
        if sweep < ITERS - 1:
            edge, inner = scaling = heat_step("scaling", edge, inner, potential, scaling)
        else:
            edge, inner, sums = heat_step("last", edge, inner, potential, scaling)
    everyone = size_x * size_z
    sums = jnp.broadcast_to(sums[None], (everyone, 1, 2 * LANES))
    sums = lax.all_to_all(sums, ("gx", "gz"), 0, 0, tiled=True).reshape(everyone, 2 * LANES)
    rho_next, ratio = call(scale_kernel, (edge, inner, sums), [(depth, width, length), (1, LANES)], scalars=0)
    return rho_next, ratio[0, :1]


def solution(mesh):
    return jax.shard_map(
        body,
        mesh=mesh,
        in_specs=(P("gz", "gx", None), P("gz", "gx", None)),
        out_specs=(P("gz", "gx", None), P()),
        check_vma=False,
    )
```

```python
import functools

import jax
import jax.numpy as jnp
import numpy as np
from jax import lax
from jax.experimental import pallas as pl
from jax.experimental.pallas import tpu as pltpu
from jax.sharding import PartitionSpec as P


HALF = 8
ITERS = 3
NEWTON = 6
LANES = 128


EDGE, INNER = (0, 3), (1, 2)


def scale():
    offsets = np.arange(-HALF, HALF + 1)
    return float(np.sum(np.exp(-2.0 * offsets * offsets / (HALF * HALF))))


def weight(gap):
    gap = gap.astype(jnp.float32)
    raw = jnp.exp(-2.0 * gap * gap / (HALF * HALF)) / scale()
    return jnp.where(jnp.abs(gap) <= HALF, raw, 0.0)


def inside_mass(cell, whole):
    total = jnp.zeros(cell.shape, jnp.float32)
    for gap in range(-HALF, HALF + 1):
        share = float(np.exp(-2.0 * gap * gap / (HALF * HALF)) / scale())
        total += jnp.where((cell + gap >= 0) & (cell + gap < whole), share, 0.0)
    return total


def split(value):
    high = value.astype(jnp.bfloat16)
    return high, (value - high.astype(jnp.float32)).astype(jnp.bfloat16)


def dot3(left, right):
    dot = functools.partial(jnp.dot, preferred_element_type=jnp.float32)
    return dot(left[0], right[0]) + (dot(left[0], right[1]) + dot(left[1], right[0]))


def iota(shape, dim):
    return lax.broadcasted_iota(jnp.int32, shape, dim)


def swap(value, axis, first):
    size = lax.axis_size(axis)
    pairs = [(i, i + 1) for i in range(first, size - 1, 2)]
    return lax.ppermute(value, axis, pairs + [(j, i) for i, j in pairs])


def group(ref, at):
    return ref[:, at * HALF : (at + 1) * HALF, :]


def groups(ref, which):
    return jnp.concatenate([group(ref, at).reshape(-1, ref.shape[2]) for at in which], axis=0)


def tables_kernel(depth, where, z_high, z_low, x_high, x_low, side_high, side_low, y_high, y_low):
    even = where[1]
    shape = z_high.shape
    rows = shape[0]
    row, col = iota(shape, 0), iota(shape, 1)
    block, cell = col // rows, col % rows
    far = jnp.where(even == 1, -depth, depth)
    gap = row // HALF - cell // HALF - jnp.where(block == 0, 0, jnp.where(block == 1, far, -far))
    z_high[...], z_low[...] = split(jnp.where(row % HALF == cell % HALF, weight(gap), 0.0))
    shape = x_high.shape
    row, col = iota(shape, 0), iota(shape, 1)
    gap = row % HALF - col % HALF + HALF * (row // rows - col // rows)
    same = row % rows // HALF == col % rows // HALF
    x_high[...], x_low[...] = split(jnp.where(same, weight(gap), 0.0))
    shape = side_high.shape
    row, col = iota(shape, 0), iota(shape, 1)
    gap = row % HALF - col % HALF + jnp.where(row < rows, HALF, -HALF)
    side_high[...], side_low[...] = split(jnp.where(row % rows // HALF == col // HALF, weight(gap), 0.0))
    shape = y_high.shape
    y_high[...], y_low[...] = split(weight(iota(shape, 0) - iota(shape, 1)))


def first_kernel(sizes, where, rho_prev, edge, inner):
    depth, _, length = rho_prev.shape
    whole_x, whole_z = sizes
    mass_z = inside_mass(where[3] + iota((depth, LANES), 0), whole_z)
    mass_y = inside_mass(iota((1, length), 1), length)
    rows = depth * HALF
    for ref, which in ((edge, EDGE), (inner, INNER)):
        for place, at in enumerate(which):
            mass_x = inside_mass(where[2] + at * HALF + iota((HALF, LANES), 0), whole_x)
            for z in range(depth):
                mass = (mass_x[:, :1] * mass_z[z : z + 1, :1]) * mass_y
                start = place * rows + z * HALF
                ref[start : start + HALF] = rho_prev[z, at * HALF : (at + 1) * HALF, :] / mass


def zy(own, far, near, z_high, z_low, y_high, y_low, high, low):
    rows = z_high.shape[0]
    results = []
    for place in range(2):
        span = slice(place * rows, (place + 1) * rows)
        for block, ref in enumerate((own, far, near)):
            to = slice((3 * place + block) * rows, (3 * place + block + 1) * rows)
            high[to], low[to] = split(ref[span])
        at = slice(3 * place * rows, 3 * (place + 1) * rows)
        results.append(dot3((z_high[...], z_low[...]), (high[at], low[at])))
    return dot3(split(jnp.concatenate(results, axis=0)), (y_high[...], y_low[...]))


def edge_kernel(where, own, far, near, z_high, z_low, y_high, y_low, send1, send0, high, low):
    value = zy(own, far, near, z_high, z_low, y_high, y_low, high, low)
    rows = value.shape[0] // 2
    before, after = value[:rows], value[rows:]
    send0[...] = jnp.where(where[0] == 1, after, before)
    send1[...] = jnp.where(where[0] == 1, before, after)


def prox(target):
    current = target
    for _ in range(NEWTON):
        grown = 0.5 * jnp.exp(current)
        current = (grown * (current - 1.0) + target) / (1.0 + grown)
    return jnp.exp(current)


def finish(kind, value, which, whole, scaling):
    if kind == "dual":
        return groups(whole, which) / value
    inner = value if scaling is None else scaling[...] * value
    rho = prox(jnp.log(inner) - groups(whole, which))
    return rho if kind == "last" else rho / value


def lane_sums(value):
    rows = jnp.sum(value, axis=0, keepdims=True)
    return sum(rows[:, i : i + LANES] for i in range(0, rows.shape[1], LANES))


def inner_kernel(kind, started, where, send1, send0, own, far, near, z_high, z_low, y_high, y_low, x_high, x_low, whole, *rest):
    scaling = None
    if started:
        scaling, *rest = rest
    if kind == "last":
        rho_prev, out, part, sums, high, low, zy_high, zy_low = rest
    else:
        out, part, high, low, zy_high, zy_low = rest
    rows = z_high.shape[0]
    value = zy(own, far, near, z_high, z_low, y_high, y_low, high, low)
    before = jnp.where(where[0] == 1, send1[...], send0[...])
    after = jnp.where(where[0] == 1, send0[...], send1[...])
    zy_high[:rows], zy_low[:rows] = split(before)
    zy_high[rows : 3 * rows], zy_low[rows : 3 * rows] = split(value)
    zy_high[3 * rows :], zy_low[3 * rows :] = split(after)
    along_x = dot3((x_high[...], x_low[...]), (zy_high[...], zy_low[...]))
    part[:rows], part[rows:] = along_x[:rows], along_x[3 * rows :]
    result = finish(kind, along_x[rows : 3 * rows], INNER, whole, scaling)
    out[...] = result
    if kind == "last":
        depth, width, length = rho_prev.shape
        sums[:, :LANES] = lane_sums(rho_prev[...].reshape(depth * width, length))
        sums[:, LANES:] = lane_sums(result)


def outer_kernel(kind, started, where, part, recv1, recv0, side_high, side_low, whole, *rest):
    scaling = None
    if started:
        scaling, *rest = rest
    if kind == "last":
        sums_inner, out, sums = rest
    else:
        (out,) = rest
    rows = recv0.shape[0]
    before = split(jnp.where(where[0] == 1, recv1[...], recv0[...]))
    after = split(jnp.where(where[0] == 1, recv0[...], recv1[...]))
    first = part[:rows] + dot3((side_high[:rows], side_low[:rows]), before)
    second = part[rows:] + dot3((side_high[rows:], side_low[rows:]), after)
    result = finish(kind, jnp.concatenate([first, second], axis=0), EDGE, whole, scaling)
    out[...] = result
    if kind == "last":
        sums[...] = sums_inner[...]
        sums[:, LANES:] += lane_sums(result)


def scale_kernel(edge, inner, sums, out, ratio):
    totals = jnp.sum(sums[...], axis=0, keepdims=True)
    mass_prev, mass_new = jnp.sum(totals[:, :LANES]), jnp.sum(totals[:, LANES:])
    ones = jnp.ones((1, LANES), jnp.float32)
    prev, new = mass_prev * ones, mass_new * ones
    ratio[...] = new / prev
    factor = (prev / new)[:, :1]
    depth, _, length = out.shape
    rows = depth * HALF
    for ref, which in ((edge, EDGE), (inner, INNER)):
        for place, at in enumerate(which):
            value = ref[place * rows : (place + 1) * rows] * factor
            out[:, at * HALF : (at + 1) * HALF, :] = value.reshape(depth, HALF, length)


def call(kernel, inputs, shapes, scratch=(), scalars=1, dtype=jnp.float32):
    specs = [pl.BlockSpec(memory_space=pltpu.SMEM)] * scalars
    specs += [pl.BlockSpec(memory_space=pltpu.VMEM)] * (len(inputs) - scalars)
    return pl.pallas_call(
        kernel,
        out_shape=[jax.ShapeDtypeStruct(shape, dtype) for shape in shapes],
        in_specs=specs,
        out_specs=[pl.BlockSpec(memory_space=pltpu.VMEM)] * len(shapes),
        scratch_shapes=scratch,
        compiler_params=pltpu.CompilerParams(vmem_limit_bytes=20 << 20),
    )(*inputs)


def step(rho_prev, potential):
    depth, width, length = rho_prev.shape
    at_x, at_z = lax.axis_index("gx"), lax.axis_index("gz")
    size_x, size_z = lax.axis_size("gx"), lax.axis_size("gz")
    where = jnp.stack([1 - at_x % 2, 1 - at_z % 2, at_x * width, at_z * depth]).astype(jnp.int32)
    rows = depth * HALF
    one, two = (rows, length), (2 * rows, length)
    zy_scratch = [pltpu.VMEM((6 * rows, length), jnp.bfloat16)] * 2
    x_scratch = [pltpu.VMEM((4 * rows, length), jnp.bfloat16)] * 2

    first = functools.partial(first_kernel, (width * size_x, depth * size_z))
    edge, inner = call(first, (where, rho_prev), [two, two])
    table_shapes = [(rows, 3 * rows), (4 * rows, 4 * rows), (2 * rows, rows), (length, length)]
    doubled = [shape for shape in table_shapes for _ in range(2)]
    tables = call(functools.partial(tables_kernel, depth), (where,), doubled, dtype=jnp.bfloat16)
    z_table, x_table, side_table, y_table = (tuple(tables[i : i + 2]) for i in range(0, 8, 2))

    def heat_step(kind, edge, inner, whole, scaling):
        far_edge = swap(edge, "gz", 1)
        near_edge = swap(edge, "gz", 0)
        far_inner = swap(inner, "gz", 1)
        near_inner = swap(inner, "gz", 0)
        sends = call(edge_kernel, (where, edge, far_edge, near_edge, *z_table, *y_table), [one, one], zy_scratch)
        recv1 = swap(sends[0], "gx", 1)
        recv0 = swap(sends[1], "gx", 0)
        started, last = scaling is not None, kind == "last"
        inputs = (where, *sends, inner, far_inner, near_inner, *z_table, *y_table, *x_table, whole)
        more = ((scaling[1],) if started else ()) + ((rho_prev,) if last else ())
        shapes = [two, two] + ([(1, 2 * LANES)] if last else [])
        new_inner, part, *sums = call(
            functools.partial(inner_kernel, kind, started), inputs + more, shapes, zy_scratch + x_scratch
        )
        more = ((scaling[0],) if started else ()) + tuple(sums)
        shapes = [two] + ([(1, 2 * LANES)] if last else [])
        new_edge, *sums = call(
            functools.partial(outer_kernel, kind, started),
            (where, part, recv1, recv0, *side_table, whole, *more),
            shapes,
        )
        return new_edge, new_inner, *sums

    scaling = None
    for sweep in range(ITERS):
        if sweep:
            edge, inner = heat_step("dual", edge, inner, rho_prev, None)
        if sweep < ITERS - 1:
            edge, inner = scaling = heat_step("scaling", edge, inner, potential, scaling)
        else:
            edge, inner, sums = heat_step("last", edge, inner, potential, scaling)
    everyone = size_x * size_z
    sums = jnp.broadcast_to(sums[None], (everyone, 1, 2 * LANES))
    sums = lax.all_to_all(sums, ("gx", "gz"), 0, 0, tiled=True).reshape(everyone, 2 * LANES)
    rho_next, ratio = call(scale_kernel, (edge, inner, sums), [(depth, width, length), (1, LANES)], scalars=0)
    return rho_next, ratio[0, :1]


def solution(mesh):
    return jax.shard_map(
        step,
        mesh=mesh,
        in_specs=(P("gz", "gx", None), P("gz", "gx", None)),
        out_specs=(P("gz", "gx", None), P()),
        check_vma=False,
    )
```

```python
import functools

import jax
import jax.numpy as jnp
import numpy as np
from jax import lax
from jax.experimental import pallas as pl
from jax.experimental.pallas import tpu as pltpu
from jax.sharding import PartitionSpec as P


HALF = 8
ITERS = 3
NEWTON = 6
LANES = 128


EDGE, INNER = (0, 3), (1, 2)


def scale():
    offsets = np.arange(-HALF, HALF + 1)
    return float(np.sum(np.exp(-2.0 * offsets * offsets / (HALF * HALF))))


def weight(gap):
    gap = gap.astype(jnp.float32)
    raw = jnp.exp(-2.0 * gap * gap / (HALF * HALF)) / scale()
    return jnp.where(jnp.abs(gap) <= HALF, raw, 0.0)


def weights(gap):
    return float(np.exp(-2.0 * gap * gap / (HALF * HALF)) / scale())


def inside_mass(cell, whole):
    total = jnp.zeros(cell.shape, jnp.float32)
    for gap in range(-HALF, HALF + 1):
        total += jnp.where((cell + gap >= 0) & (cell + gap < whole), weights(gap), 0.0)
    return total


def split(value):
    high = value.astype(jnp.bfloat16)
    return high, (value - high.astype(jnp.float32)).astype(jnp.bfloat16)


def stacked(value):
    return jnp.concatenate(split(value), axis=0)


def product(left, right, right_low):
    dot = functools.partial(jnp.dot, preferred_element_type=jnp.float32)
    rows = left.shape[0] // 2
    both = dot(left, right)
    return both[:rows] + (both[rows:] + dot(left[:rows], right_low))


def iota(shape, dim):
    return lax.broadcasted_iota(jnp.int32, shape, dim)


def swap(value, axis, first):
    size = lax.axis_size(axis)
    pairs = [(i, i + 1) for i in range(first, size - 1, 2)]
    return lax.ppermute(value, axis, pairs + [(j, i) for i, j in pairs])


def group(ref, at):
    return ref[:, at * HALF : (at + 1) * HALF, :]


def groups(ref, which):
    return jnp.concatenate([group(ref, at).reshape(-1, ref.shape[2]) for at in which], axis=0)


def tables_kernel(x_table, first_table, last_table, y_high, y_low):
    whole = x_table.shape[1]
    rows = first_table.shape[1]
    row, col = iota((whole, whole), 0), iota((whole, whole), 1)
    gap = row % HALF - col % HALF + HALF * (row // rows - col // rows)
    same = row % rows // HALF == col % rows // HALF
    x_table[...] = stacked(jnp.where(same, weight(gap), 0.0))
    row, col = iota((rows, rows), 0), iota((rows, rows), 1)
    for ref, shift in ((first_table, HALF), (last_table, -HALF)):
        ref[...] = stacked(jnp.where(row // HALF == col // HALF, weight(row % HALF - col % HALF + shift), 0.0))
    shape = y_high.shape
    y_high[...], y_low[...] = split(weight(iota(shape, 0) - iota(shape, 1)))


def first_kernel(sizes, where, rho_prev, edge, inner):
    depth, _, length = rho_prev.shape
    whole_x, whole_z = sizes
    mass_z = inside_mass(where[3] + iota((depth, LANES), 0), whole_z)
    mass_y = inside_mass(iota((1, length), 1), length)
    rows = depth * HALF
    for ref, which in ((edge, EDGE), (inner, INNER)):
        for place, at in enumerate(which):
            mass_x = inside_mass(where[2] + at * HALF + iota((HALF, LANES), 0), whole_x)
            for z in range(depth):
                mass = (mass_x[:, :1] * mass_z[z : z + 1, :1]) * mass_y
                start = place * rows + z * HALF
                ref[start : start + HALF] = rho_prev[z, at * HALF : (at + 1) * HALF, :] / mass


def zy(even, own, far, near, y_high, y_low, lined):
    rows, length = own.shape
    rows //= 2
    depth = rows // HALF
    for place in range(2):
        span = slice(place * rows, (place + 1) * rows)
        for at in range(0, length, LANES):
            lanes = slice(at, at + LANES)
            far_part, near_part = far[span, lanes], near[span, lanes]
            before = jnp.where(even == 1, far_part, near_part)
            after = jnp.where(even == 1, near_part, far_part)
            line = [part[z * HALF : (z + 1) * HALF] for part in (before, own[span, lanes], after) for z in range(depth)]
            for z in range(depth):
                here = z + depth
                total = weights(0) * line[here]
                for gap in range(1, HALF + 1):
                    total += weights(gap) * (line[here - gap] + line[here + gap])
                to = place * rows + z * HALF
                lined[to : to + HALF, lanes] = total
    return product(stacked(lined[...]), y_high[...], y_low[...])


def edge_kernel(where, own, far, near, y_high, y_low, send1, send0, lined):
    value = zy(where[1], own, far, near, y_high, y_low, lined)
    rows = value.shape[0] // 2
    before, after = value[:rows], value[rows:]
    send0[...] = jnp.where(where[0] == 1, after, before)
    send1[...] = jnp.where(where[0] == 1, before, after)


def prox(target):
    current = target
    for _ in range(NEWTON):
        grown = 0.5 * jnp.exp(current)
        current = (grown * (current - 1.0) + target) / (1.0 + grown)
    return jnp.exp(current)


def finish(kind, value, which, whole, scaling):
    if kind == "dual":
        return groups(whole, which) / value
    inner = value if scaling is None else scaling[...] * value
    rho = prox(jnp.log(inner) - groups(whole, which))
    return rho if kind == "last" else rho / value


def lane_sums(value):
    rows = jnp.sum(value, axis=0, keepdims=True)
    return sum(rows[:, i : i + LANES] for i in range(0, rows.shape[1], LANES))


def inner_kernel(kind, started, where, send1, send0, own, far, near, y_high, y_low, x_table, whole, *rest):
    scaling = None
    if started:
        scaling, *rest = rest
    if kind == "last":
        rho_prev, out, part, sums, lined, zy_high, zy_low = rest
    else:
        out, part, lined, zy_high, zy_low = rest
    rows = send1.shape[0]
    value = zy(where[1], own, far, near, y_high, y_low, lined)
    before = jnp.where(where[0] == 1, send1[...], send0[...])
    after = jnp.where(where[0] == 1, send0[...], send1[...])
    zy_high[:rows], zy_low[:rows] = split(before)
    zy_high[rows : 3 * rows], zy_low[rows : 3 * rows] = split(value)
    zy_high[3 * rows :], zy_low[3 * rows :] = split(after)
    along_x = product(x_table[...], zy_high[...], zy_low[...])
    part[:rows], part[rows:] = along_x[:rows], along_x[3 * rows :]
    result = finish(kind, along_x[rows : 3 * rows], INNER, whole, scaling)
    out[...] = result
    if kind == "last":
        depth, width, length = rho_prev.shape
        sums[:, :LANES] = lane_sums(rho_prev[...].reshape(depth * width, length))
        sums[:, LANES:] = lane_sums(result)


def outer_kernel(kind, started, where, part, recv1, recv0, first_table, last_table, whole, *rest):
    scaling = None
    if started:
        scaling, *rest = rest
    if kind == "last":
        sums_inner, out, sums = rest
    else:
        (out,) = rest
    rows = recv0.shape[0]
    before = split(jnp.where(where[0] == 1, recv1[...], recv0[...]))
    after = split(jnp.where(where[0] == 1, recv0[...], recv1[...]))
    first = part[:rows] + product(first_table[...], *before)
    second = part[rows:] + product(last_table[...], *after)
    result = finish(kind, jnp.concatenate([first, second], axis=0), EDGE, whole, scaling)
    out[...] = result
    if kind == "last":
        sums[...] = sums_inner[...]
        sums[:, LANES:] += lane_sums(result)


def scale_kernel(edge, inner, sums, out, ratio):
    totals = jnp.sum(sums[...], axis=0, keepdims=True)
    mass_prev, mass_new = jnp.sum(totals[:, :LANES]), jnp.sum(totals[:, LANES:])
    ones = jnp.ones((1, LANES), jnp.float32)
    prev, new = mass_prev * ones, mass_new * ones
    ratio[...] = new / prev
    factor = (prev / new)[:, :1]
    depth, _, length = out.shape
    rows = depth * HALF
    for ref, which in ((edge, EDGE), (inner, INNER)):
        for place, at in enumerate(which):
            value = ref[place * rows : (place + 1) * rows] * factor
            out[:, at * HALF : (at + 1) * HALF, :] = value.reshape(depth, HALF, length)


def call(kernel, inputs, shapes, scratch=(), scalars=1, dtype=jnp.float32):
    specs = [pl.BlockSpec(memory_space=pltpu.SMEM)] * scalars
    specs += [pl.BlockSpec(memory_space=pltpu.VMEM)] * (len(inputs) - scalars)
    return pl.pallas_call(
        kernel,
        out_shape=[jax.ShapeDtypeStruct(shape, dtype) for shape in shapes],
        in_specs=specs,
        out_specs=[pl.BlockSpec(memory_space=pltpu.VMEM)] * len(shapes),
        scratch_shapes=scratch,
        compiler_params=pltpu.CompilerParams(vmem_limit_bytes=20 << 20),
    )(*inputs)


def step(rho_prev, potential):
    depth, width, length = rho_prev.shape
    at_x, at_z = lax.axis_index("gx"), lax.axis_index("gz")
    size_x, size_z = lax.axis_size("gx"), lax.axis_size("gz")
    where = jnp.stack([1 - at_x % 2, 1 - at_z % 2, at_x * width, at_z * depth]).astype(jnp.int32)
    rows = depth * HALF
    one, two = (rows, length), (2 * rows, length)
    zy_scratch = [pltpu.VMEM((2 * rows, length), jnp.float32)]
    x_scratch = [pltpu.VMEM((4 * rows, length), jnp.bfloat16)] * 2

    first = functools.partial(first_kernel, (width * size_x, depth * size_z))
    edge, inner = call(first, (where, rho_prev), [two, two])
    table_shapes = [(8 * rows, 4 * rows), (2 * rows, rows), (2 * rows, rows), (length, length), (length, length)]
    x_table, *side_table, y_high, y_low = call(tables_kernel, (), table_shapes, scalars=0, dtype=jnp.bfloat16)
    y_table = (y_high, y_low)

    def heat_step(kind, edge, inner, whole, scaling):
        far_edge = swap(edge, "gz", 1)
        near_edge = swap(edge, "gz", 0)
        far_inner = swap(inner, "gz", 1)
        near_inner = swap(inner, "gz", 0)
        sends = call(edge_kernel, (where, edge, far_edge, near_edge, *y_table), [one, one], zy_scratch)
        recv1 = swap(sends[0], "gx", 1)
        recv0 = swap(sends[1], "gx", 0)
        started, last = scaling is not None, kind == "last"
        inputs = (where, *sends, inner, far_inner, near_inner, *y_table, x_table, whole)
        more = ((scaling[1],) if started else ()) + ((rho_prev,) if last else ())
        shapes = [two, two] + ([(1, 2 * LANES)] if last else [])
        new_inner, part, *sums = call(
            functools.partial(inner_kernel, kind, started), inputs + more, shapes, zy_scratch + x_scratch
        )
        more = ((scaling[0],) if started else ()) + tuple(sums)
        shapes = [two] + ([(1, 2 * LANES)] if last else [])
        new_edge, *sums = call(
            functools.partial(outer_kernel, kind, started),
            (where, part, recv1, recv0, *side_table, whole, *more),
            shapes,
        )
        return new_edge, new_inner, *sums

    scaling = None
    for sweep in range(ITERS):
        if sweep:
            edge, inner = heat_step("dual", edge, inner, rho_prev, None)
        if sweep < ITERS - 1:
            edge, inner = scaling = heat_step("scaling", edge, inner, potential, scaling)
        else:
            edge, inner, sums = heat_step("last", edge, inner, potential, scaling)
    everyone = size_x * size_z
    sums = jnp.broadcast_to(sums[None], (everyone, 1, 2 * LANES))
    sums = lax.all_to_all(sums, ("gx", "gz"), 0, 0, tiled=True).reshape(everyone, 2 * LANES)
    rho_next, ratio = call(scale_kernel, (edge, inner, sums), [(depth, width, length), (1, LANES)], scalars=0)
    return rho_next, ratio[0, :1]


def solution(mesh):
    return jax.shard_map(
        step,
        mesh=mesh,
        in_specs=(P("gz", "gx", None), P("gz", "gx", None)),
        out_specs=(P("gz", "gx", None), P()),
        check_vma=False,
    )
```

```python
import functools

import jax
import jax.numpy as jnp
import numpy as np
from jax import lax
from jax.experimental import pallas as pl
from jax.experimental.pallas import tpu as pltpu
from jax.sharding import PartitionSpec as P


HALF = 8
ITERS = 3
NEWTON = 6
LANES = 128


EDGE, INNER = (0, 3), (1, 2)


def scale():
    offsets = np.arange(-HALF, HALF + 1)
    return float(np.sum(np.exp(-2.0 * offsets * offsets / (HALF * HALF))))


def weight(gap):
    gap = gap.astype(jnp.float32)
    raw = jnp.exp(-2.0 * gap * gap / (HALF * HALF)) / scale()
    return jnp.where(jnp.abs(gap) <= HALF, raw, 0.0)


def weights(gap):
    return float(np.exp(-2.0 * gap * gap / (HALF * HALF)) / scale())


def inside_mass(cell, whole):
    total = jnp.zeros(cell.shape, jnp.float32)
    for gap in range(-HALF, HALF + 1):
        total += jnp.where((cell + gap >= 0) & (cell + gap < whole), weights(gap), 0.0)
    return total


def split(value):
    high = value.astype(jnp.bfloat16)
    return high, (value - high.astype(jnp.float32)).astype(jnp.bfloat16)


def stacked(value):
    return jnp.concatenate(split(value), axis=0)


def product(left, right, right_low):
    dot = functools.partial(jnp.dot, preferred_element_type=jnp.float32)
    rows = left.shape[0] // 2
    both = dot(left, right)
    return both[:rows] + (both[rows:] + dot(left[:rows], right_low))


def iota(shape, dim):
    return lax.broadcasted_iota(jnp.int32, shape, dim)


def swap(value, axis, first):
    size = lax.axis_size(axis)
    pairs = [(i, i + 1) for i in range(first, size - 1, 2)]
    return lax.ppermute(value, axis, pairs + [(j, i) for i, j in pairs])


def gather_pairs(value, axis):
    size = lax.axis_size(axis)
    pairs = [[i, (i + 1) % size] for i in range(1, size, 2)]
    return lax.all_gather(value, axis, axis_index_groups=pairs, tiled=True)


def group(ref, at):
    return ref[:, at * HALF : (at + 1) * HALF, :]


def groups(ref, which):
    return jnp.concatenate([group(ref, at).reshape(-1, ref.shape[2]) for at in which], axis=0)


def tables_kernel(x_table, first_table, last_table, y_high, y_low):
    whole = x_table.shape[1]
    rows = first_table.shape[1]
    row, col = iota((whole, whole), 0), iota((whole, whole), 1)
    gap = row % HALF - col % HALF + HALF * (row // rows - col // rows)
    same = row % rows // HALF == col % rows // HALF
    x_table[...] = stacked(jnp.where(same, weight(gap), 0.0))
    row, col = iota((rows, rows), 0), iota((rows, rows), 1)
    for ref, shift in ((first_table, HALF), (last_table, -HALF)):
        ref[...] = stacked(jnp.where(row // HALF == col // HALF, weight(row % HALF - col % HALF + shift), 0.0))
    shape = y_high.shape
    y_high[...], y_low[...] = split(weight(iota(shape, 0) - iota(shape, 1)))


def first_kernel(sizes, where, rho_prev, edge, inner):
    depth, _, length = rho_prev.shape
    whole_x, whole_z = sizes
    mass_z = inside_mass(where[3] + iota((depth, LANES), 0), whole_z)
    mass_y = inside_mass(iota((1, length), 1), length)
    rows = depth * HALF
    for ref, which in ((edge, EDGE), (inner, INNER)):
        for place, at in enumerate(which):
            mass_x = inside_mass(where[2] + at * HALF + iota((HALF, LANES), 0), whole_x)
            for z in range(depth):
                mass = (mass_x[:, :1] * mass_z[z : z + 1, :1]) * mass_y
                start = place * rows + z * HALF
                ref[start : start + HALF] = rho_prev[z, at * HALF : (at + 1) * HALF, :] / mass


def zy(where, own, far, near, y_high, y_low, lined):
    even = where[1]
    rows, length = own.shape
    paired = far.shape[0] > rows
    whole = rows
    rows //= 2
    depth = rows // HALF
    for place in range(2):
        span = slice(place * rows, (place + 1) * rows)
        for at in range(0, length, LANES):
            lanes = slice(at, at + LANES)
            far_part, near_part = far[span, lanes], near[span, lanes]
            if paired:
                second = far[whole + place * rows : whole + (place + 1) * rows, lanes]
                far_part = jnp.where(where[4] == 1, jnp.where(even == 1, far_part, second), 0.0)
            before = jnp.where(even == 1, far_part, near_part)
            after = jnp.where(even == 1, near_part, far_part)
            line = [part[z * HALF : (z + 1) * HALF] for part in (before, own[span, lanes], after) for z in range(depth)]
            for z in range(depth):
                here = z + depth
                total = weights(0) * line[here]
                for gap in range(1, HALF + 1):
                    total += weights(gap) * (line[here - gap] + line[here + gap])
                to = place * rows + z * HALF
                lined[to : to + HALF, lanes] = total
    return product(stacked(lined[...]), y_high[...], y_low[...])


def edge_kernel(where, own, far, near, y_high, y_low, send1, send0, lined):
    value = zy(where, own, far, near, y_high, y_low, lined)
    rows = value.shape[0] // 2
    before, after = value[:rows], value[rows:]
    send0[...] = jnp.where(where[0] == 1, after, before)
    send1[...] = jnp.where(where[0] == 1, before, after)


def prox(target):
    current = target
    for _ in range(NEWTON):
        grown = 0.5 * jnp.exp(current)
        current = (grown * (current - 1.0) + target) / (1.0 + grown)
    return jnp.exp(current)


def finish(kind, value, which, whole, scaling):
    if kind == "dual":
        return groups(whole, which) / value
    inner = value if scaling is None else scaling[...] * value
    rho = prox(jnp.log(inner) - groups(whole, which))
    return rho if kind == "last" else rho / value


def lane_sums(value):
    rows = jnp.sum(value, axis=0, keepdims=True)
    return sum(rows[:, i : i + LANES] for i in range(0, rows.shape[1], LANES))


def inner_kernel(kind, started, where, send1, send0, own, far, near, y_high, y_low, x_table, whole, *rest):
    scaling = None
    if started:
        scaling, *rest = rest
    if kind == "last":
        rho_prev, out, part, sums, lined, zy_high, zy_low = rest
    else:
        out, part, lined, zy_high, zy_low = rest
    rows = send1.shape[0]
    value = zy(where, own, far, near, y_high, y_low, lined)
    before = jnp.where(where[0] == 1, send1[...], send0[...])
    after = jnp.where(where[0] == 1, send0[...], send1[...])
    zy_high[:rows], zy_low[:rows] = split(before)
    zy_high[rows : 3 * rows], zy_low[rows : 3 * rows] = split(value)
    zy_high[3 * rows :], zy_low[3 * rows :] = split(after)
    along_x = product(x_table[...], zy_high[...], zy_low[...])
    part[:rows], part[rows:] = along_x[:rows], along_x[3 * rows :]
    result = finish(kind, along_x[rows : 3 * rows], INNER, whole, scaling)
    out[...] = result
    if kind == "last":
        depth, width, length = rho_prev.shape
        sums[:, :LANES] = lane_sums(rho_prev[...].reshape(depth * width, length))
        sums[:, LANES:] = lane_sums(result)


def outer_kernel(kind, started, where, part, recv1, recv0, first_table, last_table, whole, *rest):
    scaling = None
    if started:
        scaling, *rest = rest
    if kind == "last":
        sums_inner, out, sums = rest
    else:
        (out,) = rest
    rows = recv0.shape[0]
    before = split(jnp.where(where[0] == 1, recv1[...], recv0[...]))
    after = split(jnp.where(where[0] == 1, recv0[...], recv1[...]))
    first = part[:rows] + product(first_table[...], *before)
    second = part[rows:] + product(last_table[...], *after)
    result = finish(kind, jnp.concatenate([first, second], axis=0), EDGE, whole, scaling)
    out[...] = result
    if kind == "last":
        sums[...] = sums_inner[...]
        sums[:, LANES:] += lane_sums(result)


def scale_kernel(edge, inner, sums, out, ratio):
    totals = jnp.sum(sums[...], axis=0, keepdims=True)
    mass_prev, mass_new = jnp.sum(totals[:, :LANES]), jnp.sum(totals[:, LANES:])
    ones = jnp.ones((1, LANES), jnp.float32)
    prev, new = mass_prev * ones, mass_new * ones
    ratio[...] = new / prev
    factor = (prev / new)[:, :1]
    depth, _, length = out.shape
    rows = depth * HALF
    for ref, which in ((edge, EDGE), (inner, INNER)):
        for place, at in enumerate(which):
            value = ref[place * rows : (place + 1) * rows] * factor
            out[:, at * HALF : (at + 1) * HALF, :] = value.reshape(depth, HALF, length)


def call(kernel, inputs, shapes, scratch=(), scalars=1, dtype=jnp.float32):
    specs = [pl.BlockSpec(memory_space=pltpu.SMEM)] * scalars
    specs += [pl.BlockSpec(memory_space=pltpu.VMEM)] * (len(inputs) - scalars)
    return pl.pallas_call(
        kernel,
        out_shape=[jax.ShapeDtypeStruct(shape, dtype) for shape in shapes],
        in_specs=specs,
        out_specs=[pl.BlockSpec(memory_space=pltpu.VMEM)] * len(shapes),
        scratch_shapes=scratch,
        compiler_params=pltpu.CompilerParams(vmem_limit_bytes=20 << 20),
    )(*inputs)


def step(rho_prev, potential):
    depth, width, length = rho_prev.shape
    at_x, at_z = lax.axis_index("gx"), lax.axis_index("gz")
    size_x, size_z = lax.axis_size("gx"), lax.axis_size("gz")
    inside = (at_z > 0) & (at_z < size_z - 1)
    where = jnp.stack([1 - at_x % 2, 1 - at_z % 2, at_x * width, at_z * depth, inside]).astype(jnp.int32)
    rows = depth * HALF
    one, two = (rows, length), (2 * rows, length)
    zy_scratch = [pltpu.VMEM((2 * rows, length), jnp.float32)]
    x_scratch = [pltpu.VMEM((4 * rows, length), jnp.bfloat16)] * 2

    first = functools.partial(first_kernel, (width * size_x, depth * size_z))
    edge, inner = call(first, (where, rho_prev), [two, two])
    table_shapes = [(8 * rows, 4 * rows), (2 * rows, rows), (2 * rows, rows), (length, length), (length, length)]
    x_table, *side_table, y_high, y_low = call(tables_kernel, (), table_shapes, scalars=0, dtype=jnp.bfloat16)
    y_table = (y_high, y_low)

    def heat_step(kind, edge, inner, whole, scaling):
        near_edge = swap(edge, "gz", 0)
        far_edge = gather_pairs(edge, "gz")
        far_inner = swap(inner, "gz", 1)
        near_inner = swap(inner, "gz", 0)
        sends = call(edge_kernel, (where, edge, far_edge, near_edge, *y_table), [one, one], zy_scratch)
        recv1 = swap(sends[0], "gx", 1)
        recv0 = swap(sends[1], "gx", 0)
        started, last = scaling is not None, kind == "last"
        inputs = (where, *sends, inner, far_inner, near_inner, *y_table, x_table, whole)
        more = ((scaling[1],) if started else ()) + ((rho_prev,) if last else ())
        shapes = [two, two] + ([(1, 2 * LANES)] if last else [])
        new_inner, part, *sums = call(
            functools.partial(inner_kernel, kind, started), inputs + more, shapes, zy_scratch + x_scratch
        )
        more = ((scaling[0],) if started else ()) + tuple(sums)
        shapes = [two] + ([(1, 2 * LANES)] if last else [])
        new_edge, *sums = call(
            functools.partial(outer_kernel, kind, started),
            (where, part, recv1, recv0, *side_table, whole, *more),
            shapes,
        )
        return new_edge, new_inner, *sums

    scaling = None
    for sweep in range(ITERS):
        if sweep:
            edge, inner = heat_step("dual", edge, inner, rho_prev, None)
        if sweep < ITERS - 1:
            edge, inner = scaling = heat_step("scaling", edge, inner, potential, scaling)
        else:
            edge, inner, sums = heat_step("last", edge, inner, potential, scaling)
    everyone = size_x * size_z
    sums = jnp.broadcast_to(sums[None], (everyone, 1, 2 * LANES))
    sums = lax.all_to_all(sums, ("gx", "gz"), 0, 0, tiled=True).reshape(everyone, 2 * LANES)
    rho_next, ratio = call(scale_kernel, (edge, inner, sums), [(depth, width, length), (1, LANES)], scalars=0)
    return rho_next, ratio[0, :1]


def solution(mesh):
    return jax.shard_map(
        step,
        mesh=mesh,
        in_specs=(P("gz", "gx", None), P("gz", "gx", None)),
        out_specs=(P("gz", "gx", None), P()),
        check_vma=False,
    )
```

```python
import functools

import jax
import jax.numpy as jnp
import numpy as np
from jax import lax
from jax.experimental import pallas as pl
from jax.experimental.pallas import tpu as pltpu
from jax.sharding import PartitionSpec as P


HALF = 8
ITERS = 3
NEWTON = 6
LANES = 128


GROUPS = 4


def scale():
    offsets = np.arange(-HALF, HALF + 1)
    return float(np.sum(np.exp(-2.0 * offsets * offsets / (HALF * HALF))))


def weight(gap):
    gap = gap.astype(jnp.float32)
    raw = jnp.exp(-2.0 * gap * gap / (HALF * HALF)) / scale()
    return jnp.where(jnp.abs(gap) <= HALF, raw, 0.0)


def weights(gap):
    return float(np.exp(-2.0 * gap * gap / (HALF * HALF)) / scale())


def inside_mass(cell, whole):
    total = jnp.zeros(cell.shape, jnp.float32)
    for gap in range(-HALF, HALF + 1):
        total += jnp.where((cell + gap >= 0) & (cell + gap < whole), weights(gap), 0.0)
    return total


def split(value):
    high = value.astype(jnp.bfloat16)
    return high, (value - high.astype(jnp.float32)).astype(jnp.bfloat16)


def stacked(value):
    return jnp.concatenate(split(value), axis=0)


def product(left, right, right_low):
    dot = functools.partial(jnp.dot, preferred_element_type=jnp.float32)
    rows = left.shape[0] // 2
    both = dot(left, right)
    return both[:rows] + (both[rows:] + dot(left[:rows], right_low))


def iota(shape, dim):
    return lax.broadcasted_iota(jnp.int32, shape, dim)


def swap(value, axis, first):
    size = lax.axis_size(axis)
    pairs = [(i, i + 1) for i in range(first, size - 1, 2)]
    return lax.ppermute(value, axis, pairs + [(j, i) for i, j in pairs])


def cells(where, at):
    start = jnp.where(where[0] == 1, at, GROUPS - 1 - at) * HALF
    return pl.ds(pl.multiple_of(start, HALF), HALF)


def tables_kernel(where, x_table, first_table, last_table, y_high, y_low):
    sign = jnp.where(where[0] == 1, 1, -1)
    whole = x_table.shape[1]
    rows = first_table.shape[1]
    row, col = iota((whole, whole), 0), iota((whole, whole), 1)
    gap = row % HALF - col % HALF + sign * HALF * (row // rows - col // rows)
    same = row % rows // HALF == col % rows // HALF
    x_table[...] = stacked(jnp.where(same, weight(gap), 0.0))
    row, col = iota((rows, rows), 0), iota((rows, rows), 1)
    for ref, shift in ((first_table, sign * HALF), (last_table, -sign * HALF)):
        ref[...] = stacked(jnp.where(row // HALF == col // HALF, weight(row % HALF - col % HALF + shift), 0.0))
    shape = y_high.shape
    y_high[...], y_low[...] = split(weight(iota(shape, 0) - iota(shape, 1)))


def order_kernel(where, rho_prev, potential, rho_ordered, potential_ordered):
    depth, _, length = rho_prev.shape
    rows = depth * HALF
    for source, ref in ((rho_prev, rho_ordered), (potential, potential_ordered)):
        for at in range(GROUPS):
            ref[at * rows : (at + 1) * rows] = source[:, cells(where, at), :].reshape(rows, length)


def first_kernel(sizes, where, rho_prev, first, rest):
    depth, _, length = rho_prev.shape
    whole_x, whole_z = sizes
    mass_z = inside_mass(where[3] + iota((depth, LANES), 0), whole_z)
    mass_y = inside_mass(iota((1, length), 1), length)
    rows = depth * HALF
    for at in range(GROUPS):
        span = cells(where, at)
        mass_x = inside_mass(where[2] + span.start + iota((HALF, LANES), 0), whole_x)
        ref, base = (rest, (at - 1) * rows) if at else (first, 0)
        for z in range(depth):
            mass = (mass_x[:, :1] * mass_z[z : z + 1, :1]) * mass_y
            start = base + z * HALF
            ref[start : start + HALF] = rho_prev[z, span, :] / mass


def zy(depth, where, own, far, near, y_high, y_low, lined):
    even = where[1]
    length = own.shape[1]
    rows = depth * HALF
    for start in range(0, own.shape[0], rows):
        span = slice(start, start + rows)
        for at in range(0, length, LANES):
            lanes = slice(at, at + LANES)
            far_part, near_part = far[span, lanes], near[span, lanes]
            before = jnp.where(even == 1, far_part, near_part)
            after = jnp.where(even == 1, near_part, far_part)
            line = [part[z * HALF : (z + 1) * HALF] for part in (before, own[span, lanes], after) for z in range(depth)]
            for z in range(depth):
                here = z + depth
                total = weights(0) * line[here]
                for gap in range(1, HALF + 1):
                    total += weights(gap) * (line[here - gap] + line[here + gap])
                to = start + z * HALF
                lined[to : to + HALF, lanes] = total
    return product(stacked(lined[...]), y_high[...], y_low[...])


def zy_first_kernel(depth, where, own, far, near, y_high, y_low, out, lined):
    out[...] = zy(depth, where, own, far, near, y_high, y_low, lined)


def zy_rest_kernel(depth, where, own, far, near, y_high, y_low, inner, last, lined):
    value = zy(depth, where, own, far, near, y_high, y_low, lined)
    rows = last.shape[0]
    inner[...], last[...] = value[:-rows], value[-rows:]


def prox(target):
    current = target
    for _ in range(NEWTON):
        grown = 0.5 * jnp.exp(current)
        current = (grown * (current - 1.0) + target) / (1.0 + grown)
    return jnp.exp(current)


def finish(kind, value, span, whole, scaling):
    if kind == "dual":
        return whole[span] / value
    inner = value if scaling is None else scaling[...] * value
    rho = prox(jnp.log(inner) - whole[span])
    return rho if kind == "last" else rho / value


def lane_sums(value):
    rows = jnp.sum(value, axis=0, keepdims=True)
    return sum(rows[:, i : i + LANES] for i in range(0, rows.shape[1], LANES))


def rest_kernel(kind, started, first, inner, last, recv0, x_table, last_table, whole, *rest):
    scaling = None
    if started:
        scaling, *rest = rest
    if kind == "last":
        rho_prev, out, part, sums, high, low = rest
    else:
        out, part, high, low = rest
    rows = first.shape[0]
    at = 0
    for ref in (first, inner, last):
        span = slice(at, at + ref.shape[0])
        high[span], low[span] = split(ref[...])
        at = span.stop
    along_x = product(x_table[...], high[...], low[...])
    part[...] = along_x[:rows]
    final = along_x[3 * rows :] + product(last_table[...], *split(recv0[...]))
    value = jnp.concatenate([along_x[rows : 3 * rows], final], axis=0)
    result = finish(kind, value, slice(rows, 4 * rows), whole, scaling)
    out[...] = result
    if kind == "last":
        sums[:, :LANES] = lane_sums(rho_prev[...])
        sums[:, LANES:] = lane_sums(result)


def first_group_kernel(kind, started, part, recv1, first_table, whole, *rest):
    scaling = None
    if started:
        scaling, *rest = rest
    if kind == "last":
        sums_rest, out, sums = rest
    else:
        (out,) = rest
    value = part[...] + product(first_table[...], *split(recv1[...]))
    result = finish(kind, value, slice(0, value.shape[0]), whole, scaling)
    out[...] = result
    if kind == "last":
        sums[...] = sums_rest[...]
        sums[:, LANES:] += lane_sums(result)


def scale_kernel(where, first, rest, sums, out, ratio):
    totals = jnp.sum(sums[...], axis=0, keepdims=True)
    mass_prev, mass_new = jnp.sum(totals[:, :LANES]), jnp.sum(totals[:, LANES:])
    ones = jnp.ones((1, LANES), jnp.float32)
    prev, new = mass_prev * ones, mass_new * ones
    ratio[...] = new / prev
    factor = (prev / new)[:, :1]
    depth, _, length = out.shape
    rows = first.shape[0]
    for at in range(GROUPS):
        value = rest[(at - 1) * rows : at * rows] if at else first[...]
        out[:, cells(where, at), :] = (value * factor).reshape(depth, HALF, length)


def call(kernel, inputs, shapes, scratch=(), scalars=1, dtype=jnp.float32):
    specs = [pl.BlockSpec(memory_space=pltpu.SMEM)] * scalars
    specs += [pl.BlockSpec(memory_space=pltpu.VMEM)] * (len(inputs) - scalars)
    return pl.pallas_call(
        kernel,
        out_shape=[jax.ShapeDtypeStruct(shape, dtype) for shape in shapes],
        in_specs=specs,
        out_specs=[pl.BlockSpec(memory_space=pltpu.VMEM)] * len(shapes),
        scratch_shapes=scratch,
        compiler_params=pltpu.CompilerParams(vmem_limit_bytes=20 << 20),
    )(*inputs)


def step(rho_prev, potential):
    depth, width, length = rho_prev.shape
    at_x, at_z = lax.axis_index("gx"), lax.axis_index("gz")
    size_x, size_z = lax.axis_size("gx"), lax.axis_size("gz")
    where = jnp.stack([1 - at_x % 2, 1 - at_z % 2, at_x * width, at_z * depth]).astype(jnp.int32)
    rows = depth * HALF
    one, three, whole = (rows, length), (3 * rows, length), (4 * rows, length)
    halves = [pltpu.VMEM(whole, jnp.bfloat16)] * 2

    start = functools.partial(first_kernel, (width * size_x, depth * size_z))
    first, rest = call(start, (where, rho_prev), [one, three])
    table_shapes = [(8 * rows, 4 * rows), (2 * rows, rows), (2 * rows, rows), (length, length), (length, length)]
    x_table, first_table, last_table, *y_table = call(tables_kernel, (where,), table_shapes, dtype=jnp.bfloat16)
    rho_ordered, potential_ordered = call(order_kernel, (where, rho_prev, potential), [whole, whole])

    def heat_step(kind, first, rest, whole, scaling):
        started, last = scaling is not None, kind == "last"
        far = swap(first, "gz", 1)
        near = swap(first, "gz", 0)
        far_rest = swap(rest, "gz", 1)
        near_rest = swap(rest, "gz", 0)
        inner, send0 = call(
            functools.partial(zy_rest_kernel, depth),
            (where, rest, far_rest, near_rest, *y_table),
            [(2 * rows, length), one],
            [pltpu.VMEM(three, jnp.float32)],
        )
        recv0 = swap(send0, "gx", 0)
        (send1,) = call(
            functools.partial(zy_first_kernel, depth),
            (where, first, far, near, *y_table),
            [one],
            [pltpu.VMEM(one, jnp.float32)],
        )
        recv1 = swap(send1, "gx", 1)
        more = ((scaling[1],) if started else ()) + ((rho_ordered,) if last else ())
        total = [(1, 2 * LANES)] if last else []
        new_rest, part, *sums = call(
            functools.partial(rest_kernel, kind, started),
            (send1, inner, send0, recv0, x_table, last_table, whole, *more),
            [three, one] + total,
            halves,
            0,
        )
        more = ((scaling[0],) if started else ()) + tuple(sums)
        new_first, *sums = call(
            functools.partial(first_group_kernel, kind, started),
            (part, recv1, first_table, whole, *more),
            [one] + total,
            scalars=0,
        )
        return new_first, new_rest, *sums

    scaling = None
    for sweep in range(ITERS):
        if sweep:
            first, rest = heat_step("dual", first, rest, rho_ordered, None)
        if sweep < ITERS - 1:
            first, rest = scaling = heat_step("scaling", first, rest, potential_ordered, scaling)
        else:
            first, rest, sums = heat_step("last", first, rest, potential_ordered, scaling)
    everyone = size_x * size_z
    sums = jnp.broadcast_to(sums[None], (everyone, 1, 2 * LANES))
    sums = lax.all_to_all(sums, ("gx", "gz"), 0, 0, tiled=True).reshape(everyone, 2 * LANES)
    rho_next, ratio = call(scale_kernel, (where, first, rest, sums), [(depth, width, length), (1, LANES)])
    return rho_next, ratio[0, :1]


def solution(mesh):
    return jax.shard_map(
        step,
        mesh=mesh,
        in_specs=(P("gz", "gx", None), P("gz", "gx", None)),
        out_specs=(P("gz", "gx", None), P()),
        check_vma=False,
    )
```

```python
import functools

import jax
import jax.numpy as jnp
import numpy as np
from jax import lax
from jax.experimental import pallas as pl
from jax.experimental.pallas import tpu as pltpu
from jax.sharding import PartitionSpec as P


HALF = 8
ITERS = 3
NEWTON = 6
LANES = 128


GROUPS = 4


def scale():
    offsets = np.arange(-HALF, HALF + 1)
    return float(np.sum(np.exp(-2.0 * offsets * offsets / (HALF * HALF))))


def weight(gap):
    gap = gap.astype(jnp.float32)
    raw = jnp.exp(-2.0 * gap * gap / (HALF * HALF)) / scale()
    return jnp.where(jnp.abs(gap) <= HALF, raw, 0.0)


def weights(gap):
    return float(np.exp(-2.0 * gap * gap / (HALF * HALF)) / scale())


def inside_mass(cell, whole):
    total = jnp.zeros(cell.shape, jnp.float32)
    for gap in range(-HALF, HALF + 1):
        total += jnp.where((cell + gap >= 0) & (cell + gap < whole), weights(gap), 0.0)
    return total


def split(value):
    high = value.astype(jnp.bfloat16)
    return high, (value - high.astype(jnp.float32)).astype(jnp.bfloat16)


def stacked(value):
    return jnp.concatenate(split(value), axis=0)


def product(left, right, right_low):
    dot = functools.partial(jnp.dot, preferred_element_type=jnp.float32)
    rows = left.shape[0] // 2
    both = dot(left, right)
    return both[:rows] + (both[rows:] + dot(left[:rows], right_low))


def iota(shape, dim):
    return lax.broadcasted_iota(jnp.int32, shape, dim)


def swap(value, axis, first):
    size = lax.axis_size(axis)
    pairs = [(i, i + 1) for i in range(first, size - 1, 2)]
    return lax.ppermute(value, axis, pairs + [(j, i) for i, j in pairs])


def cells(where, at):
    start = jnp.where(where[0] == 1, at, GROUPS - 1 - at) * HALF
    return pl.ds(pl.multiple_of(start, HALF), HALF)


def tables_kernel(where, x_table, first_table, last_table, y_high, y_low, across_high, across_low):
    sign = jnp.where(where[0] == 1, 1, -1)
    whole = x_table.shape[1]
    rows = first_table.shape[1]
    row, col = iota((whole, whole), 0), iota((whole, whole), 1)
    gap = row % HALF - col % HALF + sign * HALF * (row // rows - col // rows)
    same = row % rows // HALF == col % rows // HALF
    x_table[...] = stacked(jnp.where(same, weight(gap), 0.0))
    row, col = iota((rows, rows), 0), iota((rows, rows), 1)
    for ref, shift in ((first_table, sign * HALF), (last_table, -sign * HALF)):
        ref[...] = stacked(jnp.where(row // HALF == col // HALF, weight(row % HALF - col % HALF + shift), 0.0))
    shape = y_high.shape
    row, col = iota(shape, 0), iota(shape, 1)
    y_high[...], y_low[...] = split(weight(row - col))
    other = (row < shape[0] // 2) != (col < shape[0] // 2)
    across_high[...], across_low[...] = split(jnp.where(other, weight(row - col), 0.0))


def along_y(value, y_high, y_low, across_high, across_low):
    dot = functools.partial(jnp.dot, preferred_element_type=jnp.float32)
    rows, length = value.shape
    half, quarter = length // 2, length // 4
    high, low = split(value)
    left, right, middle = slice(0, half), slice(half, length), slice(quarter, half + quarter)
    highs = jnp.concatenate([high[:, left], high[:, right]], axis=0)
    lows = jnp.concatenate([low[:, left], low[:, right]], axis=0)
    both = dot(jnp.concatenate([highs, lows], axis=0), y_high[...])
    inside = both[: 2 * rows] + (both[2 * rows :] + dot(highs, y_low[...]))
    both = dot(jnp.concatenate([high[:, middle], low[:, middle]], axis=0), across_high[...])
    across = both[:rows] + (both[rows:] + dot(high[:, middle], across_low[...]))
    return jnp.concatenate(
        [
            inside[:rows, :quarter],
            inside[:rows, quarter:] + across[:, :quarter],
            inside[rows:, :quarter] + across[:, quarter:],
            inside[rows:, quarter:],
        ],
        axis=1,
    )


def order_kernel(where, rho_prev, potential, rho_ordered, potential_ordered):
    depth, _, length = rho_prev.shape
    rows = depth * HALF
    for source, ref in ((rho_prev, rho_ordered), (potential, potential_ordered)):
        for at in range(GROUPS):
            ref[at * rows : (at + 1) * rows] = source[:, cells(where, at), :].reshape(rows, length)


def first_kernel(sizes, which, where, rho_prev, out):
    depth, _, length = rho_prev.shape
    whole_x, whole_z = sizes
    mass_z = inside_mass(where[3] + iota((depth, LANES), 0), whole_z)
    mass_y = inside_mass(iota((1, length), 1), length)
    for place, at in enumerate(which):
        span = cells(where, at)
        mass_x = inside_mass(where[2] + span.start + iota((HALF, LANES), 0), whole_x)
        for z in range(depth):
            mass = (mass_x[:, :1] * mass_z[z : z + 1, :1]) * mass_y
            start = (place * depth + z) * HALF
            out[start : start + HALF] = rho_prev[z, span, :] / mass


def zy(depth, where, own, far, near, y_tables, lined):
    even = where[1]
    length = own.shape[1]
    rows = depth * HALF
    for start in range(0, own.shape[0], rows):
        span = slice(start, start + rows)
        for at in range(0, length, LANES):
            lanes = slice(at, at + LANES)
            far_part, near_part = far[span, lanes], near[span, lanes]
            before = jnp.where(even == 1, far_part, near_part)
            after = jnp.where(even == 1, near_part, far_part)
            line = [part[z * HALF : (z + 1) * HALF] for part in (before, own[span, lanes], after) for z in range(depth)]
            for z in range(depth):
                here = z + depth
                total = weights(0) * line[here]
                for gap in range(1, HALF + 1):
                    total += weights(gap) * (line[here - gap] + line[here + gap])
                to = start + z * HALF
                lined[to : to + HALF, lanes] = total
    return along_y(lined[...], *y_tables)


def zy_one_kernel(depth, where, own, far, near, *rest):
    *y_tables, out, lined = rest
    out[...] = zy(depth, where, own, far, near, y_tables, lined)


def zy_two_kernel(depth, where, own, far, near, *rest):
    *y_tables, out, last, lined = rest
    value = zy(depth, where, own, far, near, y_tables, lined)
    rows = last.shape[0]
    out[...], last[...] = value[:-rows], value[-rows:]


def prox(target):
    current = target
    for _ in range(NEWTON):
        grown = 0.5 * jnp.exp(current)
        current = (grown * (current - 1.0) + target) / (1.0 + grown)
    return jnp.exp(current)


def finish(kind, value, span, whole, scaling):
    if kind == "dual":
        return whole[span] / value
    inner = value if scaling is None else scaling[...] * value
    rho = prox(jnp.log(inner) - whole[span])
    return rho if kind == "last" else rho / value


def lane_sums(value):
    rows = jnp.sum(value, axis=0, keepdims=True)
    return sum(rows[:, i : i + LANES] for i in range(0, rows.shape[1], LANES))


def rest_kernel(kind, started, first, inner, last, recv0, x_table, last_table, whole, *rest):
    scaling = None
    if started:
        scaling, *rest = rest
    if kind == "last":
        rho_prev, out, part, sums, high, low = rest
    else:
        out, part, high, low = rest
    rows = first.shape[0]
    at = 0
    for ref in (first, inner, last):
        span = slice(at, at + ref.shape[0])
        high[span], low[span] = split(ref[...])
        at = span.stop
    along_x = product(x_table[...], high[...], low[...])
    part[...] = along_x[:rows]
    final = along_x[3 * rows :] + product(last_table[...], *split(recv0[...]))
    value = jnp.concatenate([along_x[rows : 3 * rows], final], axis=0)
    result = finish(kind, value, slice(rows, 4 * rows), whole, scaling)
    out[...] = result
    if kind == "last":
        sums[:, :LANES] = lane_sums(rho_prev[...])
        sums[:, LANES:] = lane_sums(result)


def first_group_kernel(kind, started, part, recv1, first_table, whole, *rest):
    scaling = None
    if started:
        scaling, *rest = rest
    if kind == "last":
        sums_rest, out, sums = rest
    else:
        (out,) = rest
    value = part[...] + product(first_table[...], *split(recv1[...]))
    result = finish(kind, value, slice(0, value.shape[0]), whole, scaling)
    out[...] = result
    if kind == "last":
        sums[...] = sums_rest[...]
        sums[:, LANES:] += lane_sums(result)


def scale_kernel(where, first, rest, sums, out, ratio):
    totals = jnp.sum(sums[...], axis=0, keepdims=True)
    mass_prev, mass_new = jnp.sum(totals[:, :LANES]), jnp.sum(totals[:, LANES:])
    ones = jnp.ones((1, LANES), jnp.float32)
    prev, new = mass_prev * ones, mass_new * ones
    ratio[...] = new / prev
    factor = (prev / new)[:, :1]
    depth, _, length = out.shape
    rows = first.shape[0]
    parts = [first] + [rest.at[at * rows : (at + 1) * rows] for at in range(GROUPS - 1)]
    for at in range(GROUPS):
        value = jnp.where(where[0] == 1, parts[at][...], parts[GROUPS - 1 - at][...])
        out[:, at * HALF : (at + 1) * HALF, :] = (value * factor).reshape(depth, HALF, length)


def call(kernel, inputs, shapes, scratch=(), scalars=1, dtype=jnp.float32):
    specs = [pl.BlockSpec(memory_space=pltpu.SMEM)] * scalars
    specs += [pl.BlockSpec(memory_space=pltpu.VMEM)] * (len(inputs) - scalars)
    return pl.pallas_call(
        kernel,
        out_shape=[jax.ShapeDtypeStruct(shape, dtype) for shape in shapes],
        in_specs=specs,
        out_specs=[pl.BlockSpec(memory_space=pltpu.VMEM)] * len(shapes),
        scratch_shapes=scratch,
        compiler_params=pltpu.CompilerParams(vmem_limit_bytes=20 << 20),
    )(*inputs)


def step(rho_prev, potential):
    depth, width, length = rho_prev.shape
    at_x, at_z = lax.axis_index("gx"), lax.axis_index("gz")
    size_x, size_z = lax.axis_size("gx"), lax.axis_size("gz")
    where = jnp.stack([1 - at_x % 2, 1 - at_z % 2, at_x * width, at_z * depth]).astype(jnp.int32)
    rows = depth * HALF
    one, two, three, whole = ((count * rows, length) for count in (1, 2, 3, 4))
    halves = [pltpu.VMEM(whole, jnp.bfloat16)] * 2

    start = functools.partial(first_kernel, (width * size_x, depth * size_z))
    (first,) = call(functools.partial(start, (0, GROUPS - 1)), (where, rho_prev), [two])
    (rest,) = call(functools.partial(start, range(1, GROUPS - 1)), (where, rho_prev), [two])
    y_shapes = [(length // 2, length // 2)] * 4
    table_shapes = [(8 * rows, 4 * rows), (2 * rows, rows), (2 * rows, rows), *y_shapes]
    x_table, first_table, last_table, *y_table = call(tables_kernel, (where,), table_shapes, dtype=jnp.bfloat16)
    rho_ordered, potential_ordered = call(order_kernel, (where, rho_prev, potential), [whole, whole])

    def heat_step(turn, kind, first, rest, whole, scaling):
        started, last = scaling is not None, kind == "last"
        far = swap(first, "gz", 1)
        near = swap(first, "gz", 0)
        far_rest = swap(rest, "gz", 1)
        near_rest = swap(rest, "gz", 0)
        kernel, shapes = (zy_one_kernel, [one]) if turn else (zy_two_kernel, [one, one])
        inputs = (where, first, far, near, *y_table)
        send1, *last_group = call(functools.partial(kernel, depth), inputs, shapes, [pltpu.VMEM(first.shape, jnp.float32)])
        kernel, shapes = (zy_two_kernel, [two, one]) if turn else (zy_one_kernel, [two])
        inputs = (where, rest, far_rest, near_rest, *y_table)
        inner, *more = call(functools.partial(kernel, depth), inputs, shapes, [pltpu.VMEM(rest.shape, jnp.float32)])
        (send0,) = last_group or more
        recv0 = swap(send0, "gx", 0)
        recv1 = swap(send1, "gx", 1)
        more = ((scaling[1],) if started else ()) + ((rho_ordered,) if last else ())
        total = [(1, 2 * LANES)] if last else []
        new_rest, part, *sums = call(
            functools.partial(rest_kernel, kind, started),
            (send1, inner, send0, recv0, x_table, last_table, whole, *more),
            [three, one] + total,
            halves,
            0,
        )
        more = ((scaling[0],) if started else ()) + tuple(sums)
        new_first, *sums = call(
            functools.partial(first_group_kernel, kind, started),
            (part, recv1, first_table, whole, *more),
            [one] + total,
            scalars=0,
        )
        return new_first, new_rest, *sums

    scaling = None
    for sweep in range(ITERS):
        if sweep:
            first, rest = heat_step(2 * sweep - 1, "dual", first, rest, rho_ordered, None)
        if sweep < ITERS - 1:
            first, rest = scaling = heat_step(2 * sweep, "scaling", first, rest, potential_ordered, scaling)
        else:
            first, rest, sums = heat_step(2 * sweep, "last", first, rest, potential_ordered, scaling)
    everyone = size_x * size_z
    sums = jnp.broadcast_to(sums[None], (everyone, 1, 2 * LANES))
    sums = lax.all_to_all(sums, ("gx", "gz"), 0, 0, tiled=True).reshape(everyone, 2 * LANES)
    rho_next, ratio = call(scale_kernel, (where, first, rest, sums), [(depth, width, length), (1, LANES)])
    return rho_next, ratio[0, :1]


def solution(mesh):
    return jax.shard_map(
        step,
        mesh=mesh,
        in_specs=(P("gz", "gx", None), P("gz", "gx", None)),
        out_specs=(P("gz", "gx", None), P()),
        check_vma=False,
    )
```

```python
import functools

import jax
import jax.numpy as jnp
import numpy as np
from jax import lax
from jax.experimental import pallas as pl
from jax.experimental.pallas import tpu as pltpu
from jax.sharding import PartitionSpec as P


HALF = 8
ITERS = 3
NEWTON = 6
LANES = 128


GROUPS = 4


def scale():
    offsets = np.arange(-HALF, HALF + 1)
    return float(np.sum(np.exp(-2.0 * offsets * offsets / (HALF * HALF))))


def weight(gap):
    gap = gap.astype(jnp.float32)
    raw = jnp.exp(-2.0 * gap * gap / (HALF * HALF)) / scale()
    return jnp.where(jnp.abs(gap) <= HALF, raw, 0.0)


def weights(gap):
    return float(np.exp(-2.0 * gap * gap / (HALF * HALF)) / scale())


def inside_mass(cell, whole):
    total = jnp.zeros(cell.shape, jnp.float32)
    for gap in range(-HALF, HALF + 1):
        total += jnp.where((cell + gap >= 0) & (cell + gap < whole), weights(gap), 0.0)
    return total


def split(value):
    high = value.astype(jnp.bfloat16)
    return high, (value - high.astype(jnp.float32)).astype(jnp.bfloat16)


def stacked(value):
    return jnp.concatenate(split(value), axis=0)


def product(left, right, right_low):
    dot = functools.partial(jnp.dot, preferred_element_type=jnp.float32)
    rows = left.shape[0] // 2
    both = dot(left, right)
    return both[:rows] + (both[rows:] + dot(left[:rows], right_low))


def even(axis):
    return lax.axis_index(axis) % 2 == 0


def iota(shape, dim):
    return lax.broadcasted_iota(jnp.int32, shape, dim)


def swap(value, axis, first):
    size = lax.axis_size(axis)
    pairs = [(i, i + 1) for i in range(first, size - 1, 2)]
    return lax.ppermute(value, axis, pairs + [(j, i) for i, j in pairs])


def cells(at):
    start = jnp.where(even("gx"), at, GROUPS - 1 - at) * HALF
    return pl.ds(pl.multiple_of(start, HALF), HALF)


def tables_kernel(x_table, first_table, last_table, y_high, y_low, across_high, across_low):
    sign = jnp.where(even("gx"), 1, -1)
    whole = x_table.shape[1]
    rows = first_table.shape[1]
    row, col = iota((whole, whole), 0), iota((whole, whole), 1)
    gap = row % HALF - col % HALF + sign * HALF * (row // rows - col // rows)
    same = row % rows // HALF == col % rows // HALF
    x_table[...] = stacked(jnp.where(same, weight(gap), 0.0))
    row, col = iota((rows, rows), 0), iota((rows, rows), 1)
    for ref, shift in ((first_table, sign * HALF), (last_table, -sign * HALF)):
        ref[...] = stacked(jnp.where(row // HALF == col // HALF, weight(row % HALF - col % HALF + shift), 0.0))
    shape = y_high.shape
    row, col = iota(shape, 0), iota(shape, 1)
    y_high[...], y_low[...] = split(weight(row - col))
    other = (row < shape[0] // 2) != (col < shape[0] // 2)
    across_high[...], across_low[...] = split(jnp.where(other, weight(row - col), 0.0))


def along_y(value, y_high, y_low, across_high, across_low):
    dot = functools.partial(jnp.dot, preferred_element_type=jnp.float32)
    rows, length = value.shape
    half, quarter = length // 2, length // 4
    high, low = split(value)
    left, right, middle = slice(0, half), slice(half, length), slice(quarter, half + quarter)
    highs = jnp.concatenate([high[:, left], high[:, right]], axis=0)
    lows = jnp.concatenate([low[:, left], low[:, right]], axis=0)
    both = dot(jnp.concatenate([highs, lows], axis=0), y_high[...])
    inside = both[: 2 * rows] + (both[2 * rows :] + dot(highs, y_low[...]))
    both = dot(jnp.concatenate([high[:, middle], low[:, middle]], axis=0), across_high[...])
    across = both[:rows] + (both[rows:] + dot(high[:, middle], across_low[...]))
    return jnp.concatenate(
        [
            inside[:rows, :quarter],
            inside[:rows, quarter:] + across[:, :quarter],
            inside[rows:, :quarter] + across[:, quarter:],
            inside[rows:, quarter:],
        ],
        axis=1,
    )


def order_kernel(rho_prev, potential, rho_ordered, potential_ordered):
    depth, _, length = rho_prev.shape
    rows = depth * HALF
    for source, ref in ((rho_prev, rho_ordered), (potential, potential_ordered)):
        for at in range(GROUPS):
            ref[at * rows : (at + 1) * rows] = source[:, cells(at), :].reshape(rows, length)


def first_kernel(sizes, which, rho_prev, out):
    depth, width, length = rho_prev.shape
    whole_x, whole_z = sizes
    mass_z = inside_mass(lax.axis_index("gz") * depth + iota((depth, LANES), 0), whole_z)
    mass_y = inside_mass(iota((1, length), 1), length)
    for place, at in enumerate(which):
        span = cells(at)
        mass_x = inside_mass(lax.axis_index("gx") * width + span.start + iota((HALF, LANES), 0), whole_x)
        for z in range(depth):
            mass = (mass_x[:, :1] * mass_z[z : z + 1, :1]) * mass_y
            start = (place * depth + z) * HALF
            out[start : start + HALF] = rho_prev[z, span, :] / mass


def zy(depth, own, far, near, y_tables, lined):
    length = own.shape[1]
    rows = depth * HALF
    near_after = even("gz")
    for start in range(0, own.shape[0], rows):
        span = slice(start, start + rows)
        for at in range(0, length, LANES):
            lanes = slice(at, at + LANES)
            far_part, near_part = far[span, lanes], near[span, lanes]
            before = jnp.where(near_after, far_part, near_part)
            after = jnp.where(near_after, near_part, far_part)
            line = [part[z * HALF : (z + 1) * HALF] for part in (before, own[span, lanes], after) for z in range(depth)]
            for z in range(depth):
                here = z + depth
                total = weights(0) * line[here]
                for gap in range(1, HALF + 1):
                    total += weights(gap) * (line[here - gap] + line[here + gap])
                to = start + z * HALF
                lined[to : to + HALF, lanes] = total
    return along_y(lined[...], *y_tables)


def zy_one_kernel(depth, own, far, near, *rest):
    *y_tables, out, lined = rest
    out[...] = zy(depth, own, far, near, y_tables, lined)


def zy_two_kernel(depth, own, far, near, *rest):
    *y_tables, out, last, lined = rest
    value = zy(depth, own, far, near, y_tables, lined)
    rows = last.shape[0]
    out[...], last[...] = value[:-rows], value[-rows:]


def prox(target):
    current = target
    for _ in range(NEWTON):
        grown = 0.5 * jnp.exp(current)
        current = (grown * (current - 1.0) + target) / (1.0 + grown)
    return jnp.exp(current)


def finish(kind, value, span, whole, scaling):
    if kind == "dual":
        return whole[span] / value
    inner = value if scaling is None else scaling[...] * value
    rho = prox(jnp.log(inner) - whole[span])
    return rho if kind == "last" else rho / value


def lane_sums(value):
    rows = jnp.sum(value, axis=0, keepdims=True)
    return sum(rows[:, i : i + LANES] for i in range(0, rows.shape[1], LANES))


def rest_kernel(kind, started, first, inner, last, recv0, x_table, last_table, whole, *rest):
    scaling = None
    if started:
        scaling, *rest = rest
    if kind == "last":
        rho_prev, out, part, sums, high, low = rest
    else:
        out, part, high, low = rest
    rows = first.shape[0]
    at = 0
    for ref in (first, inner, last):
        span = slice(at, at + ref.shape[0])
        high[span], low[span] = split(ref[...])
        at = span.stop
    along_x = product(x_table[...], high[...], low[...])
    part[...] = along_x[:rows]
    final = along_x[3 * rows :] + product(last_table[...], *split(recv0[...]))
    value = jnp.concatenate([along_x[rows : 3 * rows], final], axis=0)
    result = finish(kind, value, slice(rows, 4 * rows), whole, scaling)
    out[...] = result
    if kind == "last":
        sums[:, :LANES] = lane_sums(rho_prev[...])
        sums[:, LANES:] = lane_sums(result)


def first_group_kernel(kind, started, part, recv1, first_table, whole, *rest):
    scaling = None
    if started:
        scaling, *rest = rest
    if kind == "last":
        sums_rest, out, sums = rest
    else:
        (out,) = rest
    value = part[...] + product(first_table[...], *split(recv1[...]))
    result = finish(kind, value, slice(0, value.shape[0]), whole, scaling)
    out[...] = result
    if kind == "last":
        sums[...] = sums_rest[...]
        sums[:, LANES:] += lane_sums(result)


def scale_kernel(first, rest, sums, out, ratio):
    totals = jnp.sum(sums[...], axis=0, keepdims=True)
    mass_prev, mass_new = jnp.sum(totals[:, :LANES]), jnp.sum(totals[:, LANES:])
    ones = jnp.ones((1, LANES), jnp.float32)
    prev, new = mass_prev * ones, mass_new * ones
    ratio[...] = new / prev
    factor = (prev / new)[:, :1]
    depth, _, length = out.shape
    rows = first.shape[0]
    parts = [first] + [rest.at[at * rows : (at + 1) * rows] for at in range(GROUPS - 1)]
    for at in range(GROUPS):
        value = jnp.where(even("gx"), parts[at][...], parts[GROUPS - 1 - at][...])
        out[:, at * HALF : (at + 1) * HALF, :] = (value * factor).reshape(depth, HALF, length)


def call(kernel, inputs, shapes, scratch=(), dtype=jnp.float32):
    return pl.pallas_call(
        kernel,
        out_shape=[jax.ShapeDtypeStruct(shape, dtype) for shape in shapes],
        in_specs=[pl.BlockSpec(memory_space=pltpu.VMEM)] * len(inputs),
        out_specs=[pl.BlockSpec(memory_space=pltpu.VMEM)] * len(shapes),
        scratch_shapes=scratch,
        compiler_params=pltpu.CompilerParams(vmem_limit_bytes=20 << 20),
    )(*inputs)


def step(rho_prev, potential):
    depth, width, length = rho_prev.shape
    size_x, size_z = lax.axis_size("gx"), lax.axis_size("gz")
    rows = depth * HALF
    one, two, three, whole = ((count * rows, length) for count in (1, 2, 3, 4))
    halves = [pltpu.VMEM(whole, jnp.bfloat16)] * 2

    start = functools.partial(first_kernel, (width * size_x, depth * size_z))
    (first,) = call(functools.partial(start, (0, GROUPS - 1)), (rho_prev,), [two])
    (rest,) = call(functools.partial(start, range(1, GROUPS - 1)), (rho_prev,), [two])
    y_shapes = [(length // 2, length // 2)] * 4
    table_shapes = [(8 * rows, 4 * rows), (2 * rows, rows), (2 * rows, rows), *y_shapes]
    x_table, first_table, last_table, *y_table = call(tables_kernel, (), table_shapes, dtype=jnp.bfloat16)
    rho_ordered, potential_ordered = call(order_kernel, (rho_prev, potential), [whole, whole])

    def heat_step(turn, kind, first, rest, whole, scaling):
        started, last = scaling is not None, kind == "last"
        far = swap(first, "gz", 1)
        near = swap(first, "gz", 0)
        far_rest = swap(rest, "gz", 1)
        near_rest = swap(rest, "gz", 0)
        kernel, shapes = (zy_one_kernel, [one]) if turn else (zy_two_kernel, [one, one])
        inputs = (first, far, near, *y_table)
        send1, *last_group = call(functools.partial(kernel, depth), inputs, shapes, [pltpu.VMEM(first.shape, jnp.float32)])
        kernel, shapes = (zy_two_kernel, [two, one]) if turn else (zy_one_kernel, [two])
        inputs = (rest, far_rest, near_rest, *y_table)
        inner, *more = call(functools.partial(kernel, depth), inputs, shapes, [pltpu.VMEM(rest.shape, jnp.float32)])
        (send0,) = last_group or more
        recv0 = swap(send0, "gx", 0)
        recv1 = swap(send1, "gx", 1)
        more = ((scaling[1],) if started else ()) + ((rho_ordered,) if last else ())
        total = [(1, 2 * LANES)] if last else []
        new_rest, part, *sums = call(
            functools.partial(rest_kernel, kind, started),
            (send1, inner, send0, recv0, x_table, last_table, whole, *more),
            [three, one] + total,
            halves,
        )
        more = ((scaling[0],) if started else ()) + tuple(sums)
        new_first, *sums = call(
            functools.partial(first_group_kernel, kind, started),
            (part, recv1, first_table, whole, *more),
            [one] + total,
        )
        return new_first, new_rest, *sums

    scaling = None
    for sweep in range(ITERS):
        if sweep:
            first, rest = heat_step(2 * sweep - 1, "dual", first, rest, rho_ordered, None)
        if sweep < ITERS - 1:
            first, rest = scaling = heat_step(2 * sweep, "scaling", first, rest, potential_ordered, scaling)
        else:
            first, rest, sums = heat_step(2 * sweep, "last", first, rest, potential_ordered, scaling)
    everyone = size_x * size_z
    sums = jnp.broadcast_to(sums[None], (everyone, 1, 2 * LANES))
    sums = lax.all_to_all(sums, ("gx", "gz"), 0, 0, tiled=True).reshape(everyone, 2 * LANES)
    rho_next, ratio = call(scale_kernel, (first, rest, sums), [(depth, width, length), (1, LANES)])
    return rho_next, ratio[0, :1]


def solution(mesh):
    return jax.shard_map(
        step,
        mesh=mesh,
        in_specs=(P("gz", "gx", None), P("gz", "gx", None)),
        out_specs=(P("gz", "gx", None), P()),
        check_vma=False,
    )
```

```python
import functools

import jax
import jax.numpy as jnp
import numpy as np
from jax import lax
from jax.experimental import pallas as pl
from jax.experimental.pallas import tpu as pltpu
from jax.sharding import PartitionSpec as P


HALF = 8
ITERS = 3
NEWTON = 6
LANES = 128


GROUPS = 4


def scale():
    offsets = np.arange(-HALF, HALF + 1)
    return float(np.sum(np.exp(-2.0 * offsets * offsets / (HALF * HALF))))


def weight(gap):
    gap = gap.astype(jnp.float32)
    raw = jnp.exp(-2.0 * gap * gap / (HALF * HALF)) / scale()
    return jnp.where(jnp.abs(gap) <= HALF, raw, 0.0)


def weights(gap):
    return float(np.exp(-2.0 * gap * gap / (HALF * HALF)) / scale())


def inside_mass(cell, whole):
    total = jnp.zeros(cell.shape, jnp.float32)
    for gap in range(-HALF, HALF + 1):
        total += jnp.where((cell + gap >= 0) & (cell + gap < whole), weights(gap), 0.0)
    return total


def split(value):
    high = value.astype(jnp.bfloat16)
    return high, (value - high.astype(jnp.float32)).astype(jnp.bfloat16)


def stacked(value):
    return jnp.concatenate(split(value), axis=0)


def product(left, right, right_low):
    dot = functools.partial(jnp.dot, preferred_element_type=jnp.float32)
    rows = left.shape[0] // 2
    both = dot(left, right)
    return both[:rows] + (both[rows:] + dot(left[:rows], right_low))


def even(axis):
    return lax.axis_index(axis) % 2 == 0


def iota(shape, dim):
    return lax.broadcasted_iota(jnp.int32, shape, dim)


def swap(value, axis, first):
    size = lax.axis_size(axis)
    pairs = [(i, i + 1) for i in range(first, size - 1, 2)]
    return lax.ppermute(value, axis, pairs + [(j, i) for i, j in pairs])


def gather_pairs(value, axis):
    size = lax.axis_size(axis)
    pairs = [[i, (i + 1) % size] for i in range(1, size, 2)]
    return lax.all_gather(value, axis, axis_index_groups=pairs, tiled=True)


def cells(at):
    start = jnp.where(even("gx"), at, GROUPS - 1 - at) * HALF
    return pl.ds(pl.multiple_of(start, HALF), HALF)


def tables_kernel(x_table, first_table, last_table, y_high, y_low, across_high, across_low):
    sign = jnp.where(even("gx"), 1, -1)
    whole = x_table.shape[1]
    rows = first_table.shape[1]
    row, col = iota((whole, whole), 0), iota((whole, whole), 1)
    gap = row % HALF - col % HALF + sign * HALF * (row // rows - col // rows)
    same = row % rows // HALF == col % rows // HALF
    x_table[...] = stacked(jnp.where(same, weight(gap), 0.0))
    row, col = iota((rows, rows), 0), iota((rows, rows), 1)
    for ref, shift in ((first_table, sign * HALF), (last_table, -sign * HALF)):
        ref[...] = stacked(jnp.where(row // HALF == col // HALF, weight(row % HALF - col % HALF + shift), 0.0))
    shape = y_high.shape
    row, col = iota(shape, 0), iota(shape, 1)
    y_high[...], y_low[...] = split(weight(row - col))
    other = (row < shape[0] // 2) != (col < shape[0] // 2)
    across_high[...], across_low[...] = split(jnp.where(other, weight(row - col), 0.0))


def along_y(value, y_high, y_low, across_high, across_low):
    dot = functools.partial(jnp.dot, preferred_element_type=jnp.float32)
    rows, length = value.shape
    half, quarter = length // 2, length // 4
    high, low = split(value)
    left, right, middle = slice(0, half), slice(half, length), slice(quarter, half + quarter)
    highs = jnp.concatenate([high[:, left], high[:, right]], axis=0)
    lows = jnp.concatenate([low[:, left], low[:, right]], axis=0)
    both = dot(jnp.concatenate([highs, lows], axis=0), y_high[...])
    inside = both[: 2 * rows] + (both[2 * rows :] + dot(highs, y_low[...]))
    both = dot(jnp.concatenate([high[:, middle], low[:, middle]], axis=0), across_high[...])
    across = both[:rows] + (both[rows:] + dot(high[:, middle], across_low[...]))
    return jnp.concatenate(
        [
            inside[:rows, :quarter],
            inside[:rows, quarter:] + across[:, :quarter],
            inside[rows:, :quarter] + across[:, quarter:],
            inside[rows:, quarter:],
        ],
        axis=1,
    )


def order_kernel(rho_prev, potential, rho_ordered, potential_ordered):
    depth, _, length = rho_prev.shape
    rows = depth * HALF
    for source, ref in ((rho_prev, rho_ordered), (potential, potential_ordered)):
        for at in range(GROUPS):
            ref[at * rows : (at + 1) * rows] = source[:, cells(at), :].reshape(rows, length)


def first_kernel(sizes, which, rho_prev, out):
    depth, width, length = rho_prev.shape
    whole_x, whole_z = sizes
    mass_z = inside_mass(lax.axis_index("gz") * depth + iota((depth, LANES), 0), whole_z)
    mass_y = inside_mass(iota((1, length), 1), length)
    for place, at in enumerate(which):
        span = cells(at)
        mass_x = inside_mass(lax.axis_index("gx") * width + span.start + iota((HALF, LANES), 0), whole_x)
        for z in range(depth):
            mass = (mass_x[:, :1] * mass_z[z : z + 1, :1]) * mass_y
            start = (place * depth + z) * HALF
            out[start : start + HALF] = rho_prev[z, span, :] / mass


def zy(depth, own, far, near, y_tables, lined):
    length = own.shape[1]
    rows = depth * HALF
    near_after = even("gz")
    paired = far.shape[0] > own.shape[0]
    at_z = lax.axis_index("gz")
    inside = (at_z > 0) & (at_z < lax.axis_size("gz") - 1)
    for start in range(0, own.shape[0], rows):
        span = slice(start, start + rows)
        for at in range(0, length, LANES):
            lanes = slice(at, at + LANES)
            far_part, near_part = far[span, lanes], near[span, lanes]
            if paired:
                other = far[start + own.shape[0] : start + own.shape[0] + rows, lanes]
                far_part = jnp.where(inside, jnp.where(near_after, far_part, other), 0.0)
            before = jnp.where(near_after, far_part, near_part)
            after = jnp.where(near_after, near_part, far_part)
            line = [part[z * HALF : (z + 1) * HALF] for part in (before, own[span, lanes], after) for z in range(depth)]
            for z in range(depth):
                here = z + depth
                total = weights(0) * line[here]
                for gap in range(1, HALF + 1):
                    total += weights(gap) * (line[here - gap] + line[here + gap])
                to = start + z * HALF
                lined[to : to + HALF, lanes] = total
    return along_y(lined[...], *y_tables)


def zy_one_kernel(depth, own, far, near, *rest):
    *y_tables, out, lined = rest
    out[...] = zy(depth, own, far, near, y_tables, lined)


def zy_two_kernel(depth, own, far, near, *rest):
    *y_tables, out, last, lined = rest
    value = zy(depth, own, far, near, y_tables, lined)
    rows = last.shape[0]
    out[...], last[...] = value[:-rows], value[-rows:]


def prox(target):
    current = target
    for _ in range(NEWTON):
        grown = 0.5 * jnp.exp(current)
        current = (grown * (current - 1.0) + target) / (1.0 + grown)
    return jnp.exp(current)


def finish(kind, value, span, whole, scaling):
    if kind == "dual":
        return whole[span] / value
    inner = value if scaling is None else scaling[...] * value
    rho = prox(jnp.log(inner) - whole[span])
    return rho if kind == "last" else rho / value


def lane_sums(value):
    rows = jnp.sum(value, axis=0, keepdims=True)
    return sum(rows[:, i : i + LANES] for i in range(0, rows.shape[1], LANES))


def rest_kernel(kind, started, first, inner, last, recv0, x_table, last_table, whole, *rest):
    scaling = None
    if started:
        scaling, *rest = rest
    if kind == "last":
        rho_prev, out, part, sums, high, low = rest
    else:
        out, part, high, low = rest
    rows = first.shape[0]
    at = 0
    for ref in (first, inner, last):
        span = slice(at, at + ref.shape[0])
        high[span], low[span] = split(ref[...])
        at = span.stop
    along_x = product(x_table[...], high[...], low[...])
    part[...] = along_x[:rows]
    final = along_x[3 * rows :] + product(last_table[...], *split(recv0[...]))
    value = jnp.concatenate([along_x[rows : 3 * rows], final], axis=0)
    result = finish(kind, value, slice(rows, 4 * rows), whole, scaling)
    out[...] = result
    if kind == "last":
        sums[:, :LANES] = lane_sums(rho_prev[...])
        sums[:, LANES:] = lane_sums(result)


def first_group_kernel(kind, started, part, recv1, first_table, whole, *rest):
    scaling = None
    if started:
        scaling, *rest = rest
    if kind == "last":
        sums_rest, out, sums = rest
    else:
        (out,) = rest
    value = part[...] + product(first_table[...], *split(recv1[...]))
    result = finish(kind, value, slice(0, value.shape[0]), whole, scaling)
    out[...] = result
    if kind == "last":
        sums[...] = sums_rest[...]
        sums[:, LANES:] += lane_sums(result)


def scale_kernel(first, rest, sums, out, ratio):
    totals = jnp.sum(sums[...], axis=0, keepdims=True)
    mass_prev, mass_new = jnp.sum(totals[:, :LANES]), jnp.sum(totals[:, LANES:])
    ones = jnp.ones((1, LANES), jnp.float32)
    prev, new = mass_prev * ones, mass_new * ones
    ratio[...] = new / prev
    factor = (prev / new)[:, :1]
    depth, _, length = out.shape
    rows = first.shape[0]
    parts = [first] + [rest.at[at * rows : (at + 1) * rows] for at in range(GROUPS - 1)]
    for at in range(GROUPS):
        value = jnp.where(even("gx"), parts[at][...], parts[GROUPS - 1 - at][...])
        out[:, at * HALF : (at + 1) * HALF, :] = (value * factor).reshape(depth, HALF, length)


def call(kernel, inputs, shapes, scratch=(), dtype=jnp.float32):
    return pl.pallas_call(
        kernel,
        out_shape=[jax.ShapeDtypeStruct(shape, dtype) for shape in shapes],
        in_specs=[pl.BlockSpec(memory_space=pltpu.VMEM)] * len(inputs),
        out_specs=[pl.BlockSpec(memory_space=pltpu.VMEM)] * len(shapes),
        scratch_shapes=scratch,
        compiler_params=pltpu.CompilerParams(vmem_limit_bytes=20 << 20),
    )(*inputs)


def step(rho_prev, potential):
    depth, width, length = rho_prev.shape
    size_x, size_z = lax.axis_size("gx"), lax.axis_size("gz")
    rows = depth * HALF
    one, two, three, whole = ((count * rows, length) for count in (1, 2, 3, 4))
    halves = [pltpu.VMEM(whole, jnp.bfloat16)] * 2

    start = functools.partial(first_kernel, (width * size_x, depth * size_z))
    (first,) = call(functools.partial(start, (0, GROUPS - 1)), (rho_prev,), [two])
    (rest,) = call(functools.partial(start, range(1, GROUPS - 1)), (rho_prev,), [two])
    y_shapes = [(length // 2, length // 2)] * 4
    table_shapes = [(8 * rows, 4 * rows), (2 * rows, rows), (2 * rows, rows), *y_shapes]
    x_table, first_table, last_table, *y_table = call(tables_kernel, (), table_shapes, dtype=jnp.bfloat16)
    rho_ordered, potential_ordered = call(order_kernel, (rho_prev, potential), [whole, whole])

    def heat_step(turn, kind, first, rest, whole, scaling):
        started, last = scaling is not None, kind == "last"
        near = swap(first, "gz", 0)
        far = gather_pairs(first, "gz") if last else swap(first, "gz", 1)
        far_rest = swap(rest, "gz", 1)
        near_rest = swap(rest, "gz", 0)
        kernel, shapes = (zy_one_kernel, [one]) if turn else (zy_two_kernel, [one, one])
        inputs = (first, far, near, *y_table)
        send1, *last_group = call(functools.partial(kernel, depth), inputs, shapes, [pltpu.VMEM(first.shape, jnp.float32)])
        kernel, shapes = (zy_two_kernel, [two, one]) if turn else (zy_one_kernel, [two])
        inputs = (rest, far_rest, near_rest, *y_table)
        inner, *more = call(functools.partial(kernel, depth), inputs, shapes, [pltpu.VMEM(rest.shape, jnp.float32)])
        (send0,) = last_group or more
        recv0 = swap(send0, "gx", 0)
        recv1 = swap(send1, "gx", 1)
        more = ((scaling[1],) if started else ()) + ((rho_ordered,) if last else ())
        total = [(1, 2 * LANES)] if last else []
        new_rest, part, *sums = call(
            functools.partial(rest_kernel, kind, started),
            (send1, inner, send0, recv0, x_table, last_table, whole, *more),
            [three, one] + total,
            halves,
        )
        more = ((scaling[0],) if started else ()) + tuple(sums)
        new_first, *sums = call(
            functools.partial(first_group_kernel, kind, started),
            (part, recv1, first_table, whole, *more),
            [one] + total,
        )
        return new_first, new_rest, *sums

    scaling = None
    for sweep in range(ITERS):
        if sweep:
            first, rest = heat_step(2 * sweep - 1, "dual", first, rest, rho_ordered, None)
        if sweep < ITERS - 1:
            first, rest = scaling = heat_step(2 * sweep, "scaling", first, rest, potential_ordered, scaling)
        else:
            first, rest, sums = heat_step(2 * sweep, "last", first, rest, potential_ordered, scaling)
    everyone = size_x * size_z
    sums = jnp.broadcast_to(sums[None], (everyone, 1, 2 * LANES))
    sums = lax.all_to_all(sums, ("gx", "gz"), 0, 0, tiled=True).reshape(everyone, 2 * LANES)
    rho_next, ratio = call(scale_kernel, (first, rest, sums), [(depth, width, length), (1, LANES)])
    return rho_next, ratio[0, :1]


def solution(mesh):
    return jax.shard_map(
        step,
        mesh=mesh,
        in_specs=(P("gz", "gx", None), P("gz", "gx", None)),
        out_specs=(P("gz", "gx", None), P()),
        check_vma=False,
    )
```

```python
import functools

import jax
import jax.numpy as jnp
import numpy as np
from jax import lax
from jax.experimental import pallas as pl
from jax.experimental.pallas import tpu as pltpu
from jax.sharding import PartitionSpec as P


HALF = 8
ITERS = 3
NEWTON = 6
LANES = 128


GROUPS = 4


def scale():
    offsets = np.arange(-HALF, HALF + 1)
    return float(np.sum(np.exp(-2.0 * offsets * offsets / (HALF * HALF))))


def weight(gap):
    gap = gap.astype(jnp.float32)
    raw = jnp.exp(-2.0 * gap * gap / (HALF * HALF)) / scale()
    return jnp.where(jnp.abs(gap) <= HALF, raw, 0.0)


def weights(gap):
    return float(np.exp(-2.0 * gap * gap / (HALF * HALF)) / scale())


def inside_mass(cell, whole):
    total = jnp.zeros(cell.shape, jnp.float32)
    for gap in range(-HALF, HALF + 1):
        total += jnp.where((cell + gap >= 0) & (cell + gap < whole), weights(gap), 0.0)
    return total


def split(value):
    high = value.astype(jnp.bfloat16)
    return high, (value - high.astype(jnp.float32)).astype(jnp.bfloat16)


def stacked(value):
    return jnp.concatenate(split(value), axis=0)


def product(left, right, right_low):
    dot = functools.partial(jnp.dot, preferred_element_type=jnp.float32)
    rows = left.shape[0] // 2
    both = dot(left, right)
    return both[:rows] + (both[rows:] + dot(left[:rows], right_low))


def even(axis):
    return lax.axis_index(axis) % 2 == 0


def iota(shape, dim):
    return lax.broadcasted_iota(jnp.int32, shape, dim)


def swap(value, axis, first):
    size = lax.axis_size(axis)
    pairs = [(i, i + 1) for i in range(first, size - 1, 2)]
    return lax.ppermute(value, axis, pairs + [(j, i) for i, j in pairs])


def cells(at):
    start = jnp.where(even("gx"), at, GROUPS - 1 - at) * HALF
    return pl.ds(pl.multiple_of(start, HALF), HALF)


def tables_kernel(x_table, first_table, last_table, y_high, y_low, across_high, across_low):
    sign = jnp.where(even("gx"), 1, -1)
    whole = x_table.shape[1]
    rows = first_table.shape[1]
    row, col = iota((whole, whole), 0), iota((whole, whole), 1)
    gap = row % HALF - col % HALF + sign * HALF * (row // rows - col // rows)
    same = row % rows // HALF == col % rows // HALF
    x_table[...] = stacked(jnp.where(same, weight(gap), 0.0))
    row, col = iota((rows, rows), 0), iota((rows, rows), 1)
    for ref, shift in ((first_table, sign * HALF), (last_table, -sign * HALF)):
        ref[...] = stacked(jnp.where(row // HALF == col // HALF, weight(row % HALF - col % HALF + shift), 0.0))
    shape = y_high.shape
    row, col = iota(shape, 0), iota(shape, 1)
    y_high[...], y_low[...] = split(weight(row - col))
    other = (row < shape[0] // 2) != (col < shape[0] // 2)
    across_high[...], across_low[...] = split(jnp.where(other, weight(row - col), 0.0))


def along_y(value, y_high, y_low, across_high, across_low):
    dot = functools.partial(jnp.dot, preferred_element_type=jnp.float32)
    rows, length = value.shape
    half, quarter = length // 2, length // 4
    high, low = split(value)
    left, right, middle = slice(0, half), slice(half, length), slice(quarter, half + quarter)
    highs = jnp.concatenate([high[:, left], high[:, right]], axis=0)
    lows = jnp.concatenate([low[:, left], low[:, right]], axis=0)
    both = dot(jnp.concatenate([highs, lows], axis=0), y_high[...])
    inside = both[: 2 * rows] + (both[2 * rows :] + dot(highs, y_low[...]))
    both = dot(jnp.concatenate([high[:, middle], low[:, middle]], axis=0), across_high[...])
    across = both[:rows] + (both[rows:] + dot(high[:, middle], across_low[...]))
    return jnp.concatenate(
        [
            inside[:rows, :quarter],
            inside[:rows, quarter:] + across[:, :quarter],
            inside[rows:, :quarter] + across[:, quarter:],
            inside[rows:, quarter:],
        ],
        axis=1,
    )


def order_kernel(rho_prev, potential, rho_ordered, potential_ordered):
    depth, _, length = rho_prev.shape
    rows = depth * HALF
    for source, ref in ((rho_prev, rho_ordered), (potential, potential_ordered)):
        for at in range(GROUPS):
            ref[at * rows : (at + 1) * rows] = source[:, cells(at), :].reshape(rows, length)


def first_kernel(sizes, which, rho_prev, out):
    depth, width, length = rho_prev.shape
    whole_x, whole_z = sizes
    mass_z = inside_mass(lax.axis_index("gz") * depth + iota((depth, LANES), 0), whole_z)
    mass_y = inside_mass(iota((1, length), 1), length)
    for place, at in enumerate(which):
        span = cells(at)
        mass_x = inside_mass(lax.axis_index("gx") * width + span.start + iota((HALF, LANES), 0), whole_x)
        for z in range(depth):
            mass = (mass_x[:, :1] * mass_z[z : z + 1, :1]) * mass_y
            start = (place * depth + z) * HALF
            out[start : start + HALF] = rho_prev[z, span, :] / mass


def zy(depth, own, far, near, y_tables, lined):
    length = own.shape[1]
    rows = depth * HALF
    near_after = even("gz")
    for start in range(0, own.shape[0], rows):
        span = slice(start, start + rows)
        for at in range(0, length, LANES):
            lanes = slice(at, at + LANES)
            far_part, near_part = far[span, lanes], near[span, lanes]
            before = jnp.where(near_after, far_part, near_part)
            after = jnp.where(near_after, near_part, far_part)
            line = [part[z * HALF : (z + 1) * HALF] for part in (before, own[span, lanes], after) for z in range(depth)]
            for z in range(depth):
                here = z + depth
                total = weights(0) * line[here]
                for gap in range(1, HALF + 1):
                    total += weights(gap) * (line[here - gap] + line[here + gap])
                to = start + z * HALF
                lined[to : to + HALF, lanes] = total
    return along_y(lined[...], *y_tables)


def zy_one_kernel(depth, own, far, near, *rest):
    *y_tables, out, lined = rest
    out[...] = zy(depth, own, far, near, y_tables, lined)


def zy_two_kernel(depth, own, far, near, *rest):
    *y_tables, out, last, lined = rest
    value = zy(depth, own, far, near, y_tables, lined)
    rows = last.shape[0]
    out[...], last[...] = value[:-rows], value[-rows:]


def prox(target):
    current = target
    for _ in range(NEWTON):
        grown = 0.5 * jnp.exp(current)
        current = (grown * (current - 1.0) + target) / (1.0 + grown)
    return jnp.exp(current)


def finish(kind, value, span, whole, scaling):
    if kind == "dual":
        return whole[span] / value
    inner = value if scaling is None else scaling[...] * value
    rho = prox(jnp.log(inner) - whole[span])
    return rho if kind == "last" else rho / value


def lane_sums(value):
    rows = jnp.sum(value, axis=0, keepdims=True)
    lanes = sum(rows[:, i : i + LANES] for i in range(0, rows.shape[1], LANES))
    return lanes[:, : LANES // 2] + lanes[:, LANES // 2 :]


def rest_kernel(kind, started, first, inner, last, recv0, x_table, last_table, whole, *rest):
    scaling = None
    if started:
        scaling, *rest = rest
    if kind == "last":
        rho_prev, out, part, sums, high, low = rest
    else:
        out, part, high, low = rest
    rows = first.shape[0]
    at = 0
    for ref in (first, inner, last):
        span = slice(at, at + ref.shape[0])
        high[span], low[span] = split(ref[...])
        at = span.stop
    along_x = product(x_table[...], high[...], low[...])
    part[...] = along_x[:rows]
    final = along_x[3 * rows :] + product(last_table[...], *split(recv0[...]))
    value = jnp.concatenate([along_x[rows : 3 * rows], final], axis=0)
    result = finish(kind, value, slice(rows, 4 * rows), whole, scaling)
    out[...] = result
    if kind == "last":
        sums[...] = jnp.concatenate([lane_sums(rho_prev[...]), lane_sums(result)], axis=1)


def first_group_kernel(kind, started, part, recv1, first_table, whole, *rest):
    scaling = None
    if started:
        scaling, *rest = rest
    if kind == "last":
        sums_rest, out, sums = rest
    else:
        (out,) = rest
    value = part[...] + product(first_table[...], *split(recv1[...]))
    result = finish(kind, value, slice(0, value.shape[0]), whole, scaling)
    out[...] = result
    if kind == "last":
        new = lane_sums(result)
        sums[...] = sums_rest[...] + jnp.concatenate([jnp.zeros_like(new), new], axis=1)


def scale_kernel(first, rest, sums, out, ratio):
    totals = jnp.sum(sums[...], axis=0, keepdims=True)
    mass_prev, mass_new = jnp.sum(totals[:, : LANES // 2]), jnp.sum(totals[:, LANES // 2 :])
    ones = jnp.ones((1, LANES), jnp.float32)
    prev, new = mass_prev * ones, mass_new * ones
    ratio[...] = new / prev
    factor = (prev / new)[:, :1]
    depth, _, length = out.shape
    rows = first.shape[0]
    parts = [first] + [rest.at[at * rows : (at + 1) * rows] for at in range(GROUPS - 1)]
    for at in range(GROUPS):
        value = jnp.where(even("gx"), parts[at][...], parts[GROUPS - 1 - at][...])
        out[:, at * HALF : (at + 1) * HALF, :] = (value * factor).reshape(depth, HALF, length)


def call(kernel, inputs, shapes, scratch=(), dtype=jnp.float32):
    return pl.pallas_call(
        kernel,
        out_shape=[jax.ShapeDtypeStruct(shape, dtype) for shape in shapes],
        in_specs=[pl.BlockSpec(memory_space=pltpu.VMEM)] * len(inputs),
        out_specs=[pl.BlockSpec(memory_space=pltpu.VMEM)] * len(shapes),
        scratch_shapes=scratch,
        compiler_params=pltpu.CompilerParams(vmem_limit_bytes=20 << 20),
    )(*inputs)


def step(rho_prev, potential):
    depth, width, length = rho_prev.shape
    size_x, size_z = lax.axis_size("gx"), lax.axis_size("gz")
    rows = depth * HALF
    one, two, three, whole = ((count * rows, length) for count in (1, 2, 3, 4))
    halves = [pltpu.VMEM(whole, jnp.bfloat16)] * 2

    start = functools.partial(first_kernel, (width * size_x, depth * size_z))
    (first,) = call(functools.partial(start, (0, GROUPS - 1)), (rho_prev,), [two])
    (rest,) = call(functools.partial(start, range(1, GROUPS - 1)), (rho_prev,), [two])
    y_shapes = [(length // 2, length // 2)] * 4
    table_shapes = [(8 * rows, 4 * rows), (2 * rows, rows), (2 * rows, rows), *y_shapes]
    x_table, first_table, last_table, *y_table = call(tables_kernel, (), table_shapes, dtype=jnp.bfloat16)
    rho_ordered, potential_ordered = call(order_kernel, (rho_prev, potential), [whole, whole])

    def heat_step(turn, kind, first, rest, whole, scaling):
        started, last = scaling is not None, kind == "last"
        far = swap(first, "gz", 1)
        near = swap(first, "gz", 0)
        far_rest = swap(rest, "gz", 1)
        near_rest = swap(rest, "gz", 0)
        kernel, shapes = (zy_one_kernel, [one]) if turn else (zy_two_kernel, [one, one])
        inputs = (first, far, near, *y_table)
        send1, *last_group = call(functools.partial(kernel, depth), inputs, shapes, [pltpu.VMEM(first.shape, jnp.float32)])
        kernel, shapes = (zy_two_kernel, [two, one]) if turn else (zy_one_kernel, [two])
        inputs = (rest, far_rest, near_rest, *y_table)
        inner, *more = call(functools.partial(kernel, depth), inputs, shapes, [pltpu.VMEM(rest.shape, jnp.float32)])
        (send0,) = last_group or more
        recv0 = swap(send0, "gx", 0)
        recv1 = swap(send1, "gx", 1)
        more = ((scaling[1],) if started else ()) + ((rho_ordered,) if last else ())
        total = [(1, LANES)] if last else []
        new_rest, part, *sums = call(
            functools.partial(rest_kernel, kind, started),
            (send1, inner, send0, recv0, x_table, last_table, whole, *more),
            [three, one] + total,
            halves,
        )
        more = ((scaling[0],) if started else ()) + tuple(sums)
        new_first, *sums = call(
            functools.partial(first_group_kernel, kind, started),
            (part, recv1, first_table, whole, *more),
            [one] + total,
        )
        return new_first, new_rest, *sums

    scaling = None
    for sweep in range(ITERS):
        if sweep:
            first, rest = heat_step(2 * sweep - 1, "dual", first, rest, rho_ordered, None)
        if sweep < ITERS - 1:
            first, rest = scaling = heat_step(2 * sweep, "scaling", first, rest, potential_ordered, scaling)
        else:
            first, rest, sums = heat_step(2 * sweep, "last", first, rest, potential_ordered, scaling)
    everyone = size_x * size_z
    sums = jnp.broadcast_to(sums, (everyone, LANES))
    sums = lax.all_to_all(sums, ("gx", "gz"), 0, 0, tiled=True)
    rho_next, ratio = call(scale_kernel, (first, rest, sums), [(depth, width, length), (1, LANES)])
    return rho_next, ratio[0, :1]


def solution(mesh):
    return jax.shard_map(
        step,
        mesh=mesh,
        in_specs=(P("gz", "gx", None), P("gz", "gx", None)),
        out_specs=(P("gz", "gx", None), P()),
        check_vma=False,
    )
```
